256 devices in a mesh: gx: 8 (over z_hi, core), gy: 32 (over y, x, z_lo).
Axes of the slice: x: 4, y: 4, z: 8 (z_hi: 4, z_lo: 2; z = z_hi * 2 + z_lo), core: 2. Of those that a mesh axis runs over, the one named last changes fastest.
Arguments:
- state_start: float32 [25, 16, 32, 1024], P(None, 'gx', 'gy'), as said below
- adjoint_end: float32 [25, 16, 32, 1024], P(None, 'gx', 'gy'), may hold values from -6 to 6
- limiter_flags: int32 [3, 16, 32, 16], P(None, 'gx', 'gy'), may hold values 0 or 1
- limiter_scales: float32 [3, 16, 32, 16], P(None, 'gx', 'gy'), may hold values from 0.3 to 1
- face_codes: int32 [16, 32, 16], P('gx', 'gy'), may hold values from 0 to 63
- reaction_rates: float32 [21, 21], replicated, may hold values from 0.1 to 1
Outputs:
- state_end: float32 [25, 16, 32, 1024], P(None, 'gx', 'gy')
- adjoint_start: float32 [25, 16, 32, 1024], P(None, 'gx', 'gy')
The draws below stay inside these ranges and needn't reach their ends.
Inputs may be any that keep to these rules, and one draw needn't show every extreme that they name: `face_codes`: bits 0 to 5 of an element's code choose a reflecting wall (1) or an outflow (0) for its faces on the lower and upper ends of the grid along x, y and z. `state_start`: species densities and pressure are positive at every node.
All inputs are finite; a program needn't handle non-finite values. No bound on the sum of `limiter_flags` on one device may be relied on, other than what follows from the above.
Results may differ from the reference program's by a relative error of at most 0.0001.
Values sent between devices are 32-bit elements; how exact they have to be, the bound alone decides.
No kernel may reach another device: no remote copies, remote signals or barrier semaphores. Data moves between devices by JAX's collectives and lax.ppermute only.
A program may use at most 128 MiB of HBM per device.

```python
import math
import jax
import jax.numpy as jnp
import numpy as np
from jax import lax

SPECIES = 21
VARS = 25
NODES = 64
SECTIONS = 3
NZ = 16
NX = 16
NY = 32


def draw_state_start(key, part):
    key_species, key_velocity, key_pressure = jax.random.split(key, 3)
    column_cells = NZ * 64
    species = jnp.exp(jax.random.uniform(key_species, (SPECIES, NX, NY, column_cells), jnp.float32, jnp.log(0.02), jnp.log(0.08)))
    velocity = jax.random.uniform(key_velocity, (3, NX, NY, column_cells), jnp.float32, -0.4, 0.4)
    pressure = jax.random.uniform(key_pressure, (NX, NY, column_cells), jnp.float32, 0.7, 1.3)
    density = jnp.sum(species, axis=0)
    momenta = velocity * density
    energy = 2.5 * pressure + 0.5 * jnp.sum(momenta * momenta, axis=0) / density
    return jnp.concatenate([species, momenta, energy[None]], axis=0)


def plant(entries, stream_key, least, high):
    place = [jax.random.randint(jax.random.fold_in(stream_key, axis), (), 0, length) for axis, length in enumerate(entries.shape)]
    widest = entries.shape.index(max(entries.shape))
    beside = place[:widest] + [(place[widest] + 1) % entries.shape[widest]] + place[widest + 1:]
    return entries.at[tuple(place)].set(least).at[tuple(beside)].set(high)


def block_scale(rng, shape, pieces, low, top_value):
    loudness, own = 1.0, jax.random.fold_in(rng, 6)
    for dim, parts in pieces:
        steps = jnp.exp(jax.random.uniform(jax.random.fold_in(own, dim), (parts,), jnp.float32, low / len(pieces), top_value / len(pieces)))
        loudness = loudness * jnp.repeat(steps, shape[dim] // parts).reshape([-1 if axis == dim else 1 for axis in range(len(shape))])
    return loudness


def noise(key, dims, width, bound, cuts=(), held_as=jnp.bfloat16):
    entries = jax.random.normal(key, dims, jnp.float32) * width
    if len(cuts) > 0:
        entries = block_scale(key, dims, cuts, -0.22, 0.18) * entries
    return jnp.clip(entries, min=-bound, max=bound).astype(held_as)


def setup_inputs(seed: int = 0) -> dict:
    key_of = jax.random.split(jax.random.key(seed), 7)
    state_start = draw_state_start(jax.random.fold_in(key_of[6], 71), 0)
    adjoint_end = noise(key_of[1], (VARS, NX, NY, NZ * NODES), 1.0, 6.0, ((1, 8), (2, 32)), jnp.float32)
    limiter_flags = plant((jax.random.randint(key_of[2], (SECTIONS, NX, NY, NZ), 0, 2) < 1).astype(jnp.int32), jax.random.fold_in(key_of[2], 1), 0, 1)
    limiter_scales = jnp.clip(0.3 + 0.7 * jax.random.uniform(key_of[3], (SECTIONS, NX, NY, NZ), jnp.float32) ** block_scale(key_of[3], (SECTIONS, NX, NY, NZ), ((1, 8), (2, 32)), -0.2, 0.2), 0.3, 1.0)
    face_codes = plant(jax.random.randint(key_of[4], (NX, NY, NZ), 0, 64), jax.random.fold_in(key_of[4], 1), 0, 63).astype(jnp.int32)
    reaction_rates = jnp.clip(jnp.exp(jax.random.uniform(key_of[5], (SPECIES, SPECIES), jnp.float32, math.log(0.1), math.log(1.0))), 0.1, 1.0)
    return {"state_start": state_start, "adjoint_end": adjoint_end, "limiter_flags": limiter_flags, "limiter_scales": limiter_scales, "face_codes": face_codes, "reaction_rates": reaction_rates}


HEAT_RATIO = 1.4
time_step = 0.008
HIGHEST = lax.Precision.HIGHEST

def node_tables():
    inner_point = 1.0 / np.sqrt(5.0)
    points = np.array([-1.0, -inner_point, inner_point, 1.0])
    weights = np.array([1.0, 5.0, 5.0, 1.0]) / 6.0
    barycentric = np.array([1.0 / np.prod([points[node_index] - points[other_node] for other_node in range(4) if other_node != node_index]) for node_index in range(4)])
    deriv_matrix = np.zeros((4, 4))
    for row_node in range(4):
        for col_node in range(4):
            if row_node != col_node:
                deriv_matrix[row_node, col_node] = barycentric[col_node] / barycentric[row_node] / (points[row_node] - points[col_node])
        deriv_matrix[row_node, row_node] = -np.sum(deriv_matrix[row_node])
    gradients = np.zeros((3, 128, 128))
    selectors = np.zeros((3, 2, 512, 128))
    averaging = np.zeros((128, 128))
    for source_pos in range(128):
        source_elem, source_local = divmod(source_pos, 64)
        source_idx = (source_local // 16, source_local // 4 % 4, source_local % 4)
        for target_pos in range(128):
            target_elem, target_local = divmod(target_pos, 64)
            if source_elem != target_elem:
                continue
            target_idx = (target_local // 16, target_local // 4 % 4, target_local % 4)
            averaging[source_pos, target_pos] = weights[source_idx[0]] * weights[source_idx[1]] * weights[source_idx[2]] / 8.0
            for direction in range(3):
                if all((source_idx[other_node] == target_idx[other_node] for other_node in range(3) if other_node != direction)):
                    gradients[direction, source_pos, target_pos] = deriv_matrix[target_idx[direction], source_idx[direction]]
    for source_pos in range(512):
        source_elem, source_local = divmod(source_pos, 64)
        source_idx = (source_local // 16, source_local // 4 % 4, source_local % 4)
        for direction in range(3):
            others = [source_idx[other_node] for other_node in range(3) if other_node != direction]
            column = source_elem * 16 + others[0] * 4 + others[1]
            if source_idx[direction] == 0:
                selectors[direction, 0, source_pos, column] = 1.0
            if source_idx[direction] == 3:
                selectors[direction, 1, source_pos, column] = 1.0
    return (gradients, selectors, averaging)

def block_product(values, table):
    full_shape = values.shape
    block_size = table.shape[0]
    grouped = values.reshape(full_shape[:-1] + (full_shape[-1] // block_size, block_size))
    result = jnp.matmul(grouped, table, precision=HIGHEST)
    return result.reshape(full_shape[:-1] + (-1,))

def row_pick(variables, row, ndim, float_type):
    picked = (jnp.arange(variables, dtype=jnp.int32) == row).astype(float_type)
    return picked.reshape((variables,) + (1,) * (ndim - 1))

def physical_flux(fields, direction):
    variables = fields.shape[0]
    density = lax.optimization_barrier(jnp.sum(fields[:SPECIES], axis=0))
    inverse = 1.0 / density
    momenta = fields[SPECIES:SPECIES + 3]
    energy = fields[SPECIES + 3]
    velocity = fields[SPECIES + direction] * inverse
    pressure = (HEAT_RATIO - 1.0) * (energy - 0.5 * lax.optimization_barrier(jnp.sum(momenta * momenta, axis=0)) * inverse)
    press_row = row_pick(variables, SPECIES + direction, fields.ndim, fields.dtype)
    energy_row = row_pick(variables, variables - 1, fields.ndim, fields.dtype)
    flux_values = fields * velocity + pressure * (press_row + energy_row * velocity)
    wave_speed = jnp.sqrt(velocity * velocity + HEAT_RATIO * pressure * inverse)
    return (flux_values, wave_speed)

def face_flux(lower_state, upper_state, direction):
    lower_flux, lower_speed = physical_flux(lower_state, direction)
    upper_flux, upper_speed = physical_flux(upper_state, direction)
    shared = 0.5 * (lower_flux + upper_flux) - 0.25 * (lower_speed + upper_speed) * (upper_state - lower_state)
    return (shared, lower_flux, upper_flux)

def face_terms(low_trace, high_trace, low_ghost, high_ghost, along_axis, direction):
    extent = low_trace.shape[along_axis]
    offset = low_ghost.shape[along_axis]
    lower_side = jnp.concatenate([low_ghost, high_trace], axis=along_axis)
    upper_side = jnp.concatenate([low_trace, high_ghost], axis=along_axis)
    shared, lower_flux, upper_flux = face_flux(lower_side, upper_side, direction)
    at_low = 6.0 * (lax.slice_in_dim(shared, 0, extent, axis=along_axis) - lax.slice_in_dim(upper_flux, 0, extent, axis=along_axis))
    at_high = -6.0 * (lax.slice_in_dim(shared, offset, extent + offset, axis=along_axis) - lax.slice_in_dim(lower_flux, offset, extent + offset, axis=along_axis))
    return (at_low, at_high)

def reflect(face_state, direction, wall_factor):
    picked = row_pick(face_state.shape[0], SPECIES + direction, face_state.ndim, face_state.dtype)
    return face_state * (1.0 + picked * (wall_factor - 1.0))

def wall_sign(face_codes, bit_index, float_type):
    return (1 - 2 * (face_codes // 2 ** bit_index % 2)).astype(float_type)

def edge_traces(fields, selectors):
    variables = fields.shape[0]
    x_low = block_product(fields[:, 0], selectors[0, 0]).reshape(variables, -1)
    x_high = block_product(fields[:, -1], selectors[0, 1]).reshape(variables, -1)
    y_low = block_product(fields[:, :, 0], selectors[1, 0]).reshape(variables, -1)
    y_high = block_product(fields[:, :, -1], selectors[1, 1]).reshape(variables, -1)
    return (x_low, x_high, y_low, y_high)

def boundary_states(traces, face_codes):
    x_low, x_high, y_low, y_high = traces
    float_type = x_low.dtype
    sign_xlow = jnp.repeat(wall_sign(face_codes[0], 0, float_type), 16, axis=-1).reshape(-1)
    sign_xhigh = jnp.repeat(wall_sign(face_codes[-1], 1, float_type), 16, axis=-1).reshape(-1)
    sign_ylow = jnp.repeat(wall_sign(face_codes[:, 0], 2, float_type), 16, axis=-1).reshape(-1)
    sign_yhigh = jnp.repeat(wall_sign(face_codes[:, -1], 3, float_type), 16, axis=-1).reshape(-1)
    return (reflect(x_low, 0, sign_xlow), reflect(x_high, 0, sign_xhigh), reflect(y_low, 1, sign_ylow), reflect(y_high, 1, sign_yhigh))

def reaction_matrix(reaction_rates):
    off_diag = reaction_rates * (1.0 - jnp.eye(reaction_rates.shape[0], dtype=reaction_rates.dtype))
    return off_diag - jnp.diag(lax.optimization_barrier(jnp.sum(off_diag, axis=0)))

def residual(fields, ghosts, face_codes, coupling, gradients, selectors):
    variables, rows_x, rows_y, column_cells = fields.shape
    extra = variables - SPECIES
    padded_coupling = jnp.pad(coupling, ((0, extra), (0, extra)))
    tendency = jnp.einsum('sr,rabc->sabc', padded_coupling, fields, precision=HIGHEST)
    for direction in range(3):
        flux_values, _ = physical_flux(fields, direction)
        tendency = tendency - block_product(flux_values, gradients[direction])
    face_cells = column_cells // 4
    ghost_shapes = ((variables, 1, rows_y, face_cells), (variables, rows_x, 1, face_cells))
    for direction in range(2):
        low_trace = block_product(fields, selectors[direction, 0])
        high_trace = block_product(fields, selectors[direction, 1])
        low_ghost = ghosts[2 * direction].reshape(ghost_shapes[direction])
        high_ghost = ghosts[2 * direction + 1].reshape(ghost_shapes[direction])
        at_low, at_high = face_terms(low_trace, high_trace, low_ghost, high_ghost, direction + 1, direction)
        tendency = tendency + block_product(at_low, selectors[direction, 0].T) + block_product(at_high, selectors[direction, 1].T)
    low_trace = block_product(fields, selectors[2, 0])
    high_trace = block_product(fields, selectors[2, 1])
    low_ghost = reflect(low_trace[..., :16], 2, wall_sign(face_codes[:, :, :1], 4, fields.dtype))
    high_ghost = reflect(high_trace[..., -16:], 2, wall_sign(face_codes[:, :, -1:], 5, fields.dtype))
    at_low, at_high = face_terms(low_trace, high_trace, low_ghost, high_ghost, 3, 2)
    tendency = tendency + block_product(at_low, selectors[2, 0].T) + block_product(at_high, selectors[2, 1].T)
    return tendency

def limiter(values, section_flags, section_scales, averaging):
    damping = jnp.where(section_flags == 1, section_scales, 1.0)
    damping = jnp.repeat(damping, 64, axis=-1)
    mean_values = block_product(values, averaging)
    return mean_values + damping * (values - mean_values)

def reference(state_start, adjoint_end, limiter_flags, limiter_scales, face_codes, reaction_rates):
    tables = node_tables()
    gradients = jnp.asarray(tables[0], dtype=state_start.dtype)
    selectors = jnp.asarray(tables[1], dtype=state_start.dtype)
    averaging = jnp.asarray(tables[2], dtype=state_start.dtype)
    coupling = reaction_matrix(reaction_rates)

    def right_side(fields):
        ghosts = boundary_states(edge_traces(fields, selectors), face_codes)
        return residual(fields, ghosts, face_codes, coupling, gradients, selectors)
    right_side = jax.checkpoint(right_side)

    def forward(initial):
        section_one = limiter(initial + time_step * right_side(initial), limiter_flags[0], limiter_scales[0], averaging)
        section_two = limiter(0.75 * initial + 0.25 * (section_one + time_step * right_side(section_one)), limiter_flags[1], limiter_scales[1], averaging)
        return limiter(1.0 / 3.0 * initial + 2.0 / 3.0 * (section_two + time_step * right_side(section_two)), limiter_flags[2], limiter_scales[2], averaging)
    state_end, pullback = jax.vjp(forward, state_start)
    adjoint_start = pullback(adjoint_end)[0]
    return (state_end, adjoint_start)
```

```python
import functools

import jax
import jax.numpy as jnp
import numpy as np
from jax import lax
from jax.experimental import pallas as pl
from jax.experimental.pallas import tpu as pltpu
from jax.sharding import PartitionSpec as P

SPECIES = 21
VARS = 25
ENERGY = 24
GROUPS = 7
STEP = 0.008
F32 = jnp.float32
BF16 = jnp.bfloat16
ROWS = 16
LANES = 128


def node_tables():
    points = np.array([-1.0, -1.0 / np.sqrt(5.0), 1.0 / np.sqrt(5.0), 1.0])
    weights = np.array([1.0, 5.0, 5.0, 1.0]) / 6.0
    bary = np.array([1.0 / np.prod([points[a] - points[b] for b in range(4) if b != a]) for a in range(4)])
    deriv = np.zeros((4, 4))
    for a in range(4):
        for b in range(4):
            if a != b:
                deriv[a, b] = bary[b] / bary[a] / (points[a] - points[b])
        deriv[a, a] = -np.sum(deriv[a])
    eye = np.eye(4)
    pair = np.eye(2)
    ops = [
        np.kron(np.kron(deriv.T, eye), eye),
        np.kron(np.kron(eye, deriv.T), eye),
        np.kron(np.kron(eye, eye), deriv.T),
    ]
    grads = [np.kron(pair, op) for op in ops]
    cube = np.kron(np.kron(weights, weights), weights) / 8.0
    mean = np.kron(pair, np.repeat(cube[:, None], 64, axis=1))
    forward = np.concatenate(grads, axis=0)
    backward = np.concatenate([g.T for g in grads], axis=1)
    return forward, backward, mean, mean.T


def halves(table):
    table = np.asarray(table, np.float32)
    high = table.astype(jnp.bfloat16)
    low = (table - high.astype(np.float32)).astype(jnp.bfloat16)
    return jnp.asarray(np.stack([high, low]))


def split(values):
    high = values.astype(BF16)
    return high, (values - high.astype(F32)).astype(BF16)


def product(high, low, table):
    dot = functools.partial(jnp.dot, preferred_element_type=F32)
    return dot(high, table[0]) + dot(high, table[1]) + dot(low, table[0])


def roll(values, shift, axis):
    shift = shift % values.shape[axis]
    return values if shift == 0 else pltpu.roll(values, shift, axis)


def lane_of(rows=ROWS):
    return lax.broadcasted_iota(jnp.int32, (rows, LANES), 1)


def node_index(direction, rows=ROWS):
    return (lane_of(rows) >> (4, 2, 0)[direction]) & 3


def block(var):
    return pl.ds(ROWS * var, ROWS)


class Face:
    def __init__(self, wall, direction):
        index = node_index(direction)
        inside = wall == 0.0
        self.low = jnp.logical_and(index == 0, inside)
        self.high = jnp.logical_and(index == 3, inside)
        self.sign = jnp.where(wall < 0.0, -1.0, 1.0)
        live = jnp.where(wall > 0.0, 0.0, 1.0)
        self.three = jnp.where(index == 0, 3.0, jnp.where(index == 3, -3.0, 0.0)) * live
        self.half = jnp.where(jnp.logical_or(index == 0, index == 3), 1.5, 0.0) * live
        self.momentum = SPECIES + direction

    def outside(self, var, own, low, high):
        edge = own * self.sign if var == self.momentum else own
        return jnp.where(self.low, low, jnp.where(self.high, high, edge))


def shift_z(values):
    first = lane_of() < 64
    low = roll(values, 61, 1)
    low = jnp.where(first, roll(low, 1, 0), low)
    high = roll(values, 67, 1)
    high = jnp.where(first, high, roll(high, ROWS - 1, 0))
    return low, high


class Received:
    def __init__(self, refs, part=0):
        even_x = (jnp.zeros((8, LANES), jnp.int32) + lax.axis_index("gx") % 2) == 0
        even_y = (jnp.zeros((ROWS, LANES), jnp.int32) + lax.axis_index("gy") % 2) == 0
        xa, xb, ya, yb = refs
        self.packs = []
        for group in range(GROUPS):
            at = part * GROUPS + group
            a, b, c, d = xa[at], xb[at], ya[at], yb[at]
            self.packs.append(
                (
                    jnp.where(even_x, b, a),
                    jnp.where(even_x, a, b),
                    jnp.where(even_y, d, c),
                    jnp.where(even_y, c, d),
                )
            )

    def along_x(self, var, own):
        group, slot = divmod(var, 4)
        low, high = self.packs[group][:2]
        first, second = own[:8], own[8:]
        return (
            jnp.concatenate([roll(low, -16 * slot, 1), roll(first, -48, 1)], axis=0),
            jnp.concatenate([roll(second, 48, 1), roll(high, 16 * (3 - slot), 1)], axis=0),
        )

    def along_y(self, var):
        group, slot = divmod(var, 4)
        low, high = self.packs[group][2:]
        return roll(low, -4 * slot, 1), roll(high, 4 * (3 - slot), 1)


def pack(field, refs, part=0):
    even_x = (jnp.zeros((8, LANES), jnp.int32) + lax.axis_index("gx") % 2) == 0
    even_y = (jnp.zeros((ROWS, LANES), jnp.int32) + lax.axis_index("gy") % 2) == 0
    xa, xb, ya, yb = refs
    spot_x, spot_y = node_index(0, 8), node_index(1)

    def merged(spot, pieces):
        out = pieces[3]
        for slot in (2, 1, 0):
            out = jnp.where(spot == slot, pieces[slot], out)
        return out

    for group in range(GROUPS):
        at = part * GROUPS + group
        own = [field(min(4 * group + slot, ENERGY)) for slot in range(4)]
        if group == GROUPS - 1:
            x_low, x_high = own[0][:8], roll(own[0][8:], -48, 1)
            y_low, y_high = own[0], roll(own[0], -12, 1)
        else:
            x_low = merged(spot_x, [roll(own[s][:8], 16 * s, 1) for s in range(4)])
            x_high = merged(spot_x, [roll(own[s][8:], 16 * (s - 3), 1) for s in range(4)])
            y_low = merged(spot_y, [roll(own[s], 4 * s, 1) for s in range(4)])
            y_high = merged(spot_y, [roll(own[s], 4 * (s - 3), 1) for s in range(4)])
        xa[at] = jnp.where(even_x, x_high, x_low)
        xb[at] = jnp.where(even_x, x_low, x_high)
        ya[at] = jnp.where(even_y, y_high, y_low)
        yb[at] = jnp.where(even_y, y_low, y_high)


class Gas:
    def __init__(self, field, directions):
        density = field(0)
        for var in range(1, SPECIES):
            density = density + field(var)
        self.inverse = 1.0 / density
        self.momenta = [field(SPECIES + e) for e in range(3)]
        m0, m1, m2 = self.momenta
        self.square = m0 * m0 + m1 * m1 + m2 * m2
        self.pressure = 0.4 * (field(ENERGY) - 0.5 * self.square * self.inverse)
        self.velocity = {d: self.momenta[d] * self.inverse for d in directions}
        sound = 1.4 * self.pressure * self.inverse
        self.speed = {d: jnp.sqrt(self.velocity[d] * self.velocity[d] + sound) for d in directions}


def face_gain(face, direction, own, other):
    weight = face.half * (own.speed[direction] + other.speed[direction])
    u_in, u_out = own.velocity[direction], other.velocity[direction]
    take, leave = face.three * u_out + weight, face.three * u_in + weight

    def gain(var, inside, outside):
        total = outside * take - inside * leave
        if var == face.momentum:
            total = total + face.three * (other.pressure - own.pressure)
        if var == ENERGY:
            total = total + face.three * (other.pressure * u_out - own.pressure * u_in)
        return total

    return gain


class Back:
    def __init__(self, gas):
        self.gas = gas
        zero = jnp.zeros((ROWS, LANES), F32)
        self.speed = {}
        self.velocity = {}
        self.pressure = zero

    def flux(self, var, direction, value, cotangent):
        gas = self.gas
        term = cotangent * value
        if var == ENERGY:
            term = term + cotangent * gas.pressure
            self.pressure = self.pressure + cotangent * gas.velocity[direction]
        if var == SPECIES + direction:
            self.pressure = self.pressure + cotangent
        held = self.velocity.get(direction)
        self.velocity[direction] = term if held is None else held + term
        return cotangent * gas.velocity[direction]

    def wave(self, direction, term):
        held = self.speed.get(direction)
        self.speed[direction] = term if held is None else held + term

    def close(self):
        gas = self.gas
        inverse, pressure = gas.inverse, self.pressure
        into = jnp.zeros((ROWS, LANES), F32)
        for direction, term in self.speed.items():
            scaled = term / gas.speed[direction]
            self.velocity[direction] = self.velocity[direction] + scaled * gas.velocity[direction]
            pressure = pressure + 0.7 * scaled * inverse
            into = into + 0.7 * scaled * gas.pressure
        for direction, term in self.velocity.items():
            into = into + term * gas.momenta[direction]
        into = into - 0.2 * pressure * gas.square
        self.species = -inverse * inverse * into
        self.momentum = []
        for e in range(3):
            term = -0.4 * pressure * gas.momenta[e]
            if e in self.velocity:
                term = term + self.velocity[e]
            self.momentum.append(term * inverse)
        self.energy = 0.4 * pressure

    def rest(self, var):
        if var < SPECIES:
            return self.species
        return self.energy if var == ENERGY else self.momentum[var - SPECIES]


def spread(rows, first):
    place = lax.broadcasted_iota(jnp.int32, (8, 16), 0)
    element = lax.broadcasted_iota(jnp.int32, (8, 16), 1)
    left = lane_of(8) < 64
    columns = []
    for column in range(2):
        line = jnp.broadcast_to(rows[first + column : first + column + 1, :], (8, 16))
        picked = [
            jnp.sum(jnp.where(element == 2 * place + half, line, 0.0), axis=1, keepdims=True)
            for half in range(2)
        ]
        columns.append(jnp.where(left, picked[0], picked[1]))
    return jnp.concatenate(columns, axis=0)


def damping(flags, scales, section):
    factor = jnp.where(flags[...] == 1, scales[...], 1.0)
    return spread(factor, 2 * section)


def limited(field, factor, high, low, table, transposed):
    for var in range(VARS):
        value = field(var)
        if transposed:
            value = (1.0 - factor) * value
        high[block(var), :], low[block(var), :] = split(value)
    means = product(high[...], low[...], table)

    def get(var):
        mean = means[ROWS * var : ROWS * (var + 1)]
        if transposed:
            return factor * field(var) + mean
        return mean + factor * (field(var) - mean)

    return get


def start_kernel(state, adjoint, flags, scales, mean_t, lam, xa, xb, ya, yb, high, low):
    refs = (xa, xb, ya, yb)
    pack(lambda v: state[v], refs, 0)
    get = limited(lambda v: adjoint[v], damping(flags, scales, 2), high, low, mean_t, True)
    for var in range(VARS):
        lam[var] = (2.0 / 3.0) * get(var)
    pack(lambda v: lam[v], refs, 1)


def table_kernel(columns, lines, codes, flags, scales, walls, factors):
    for section in range(3):
        factors[section] = damping(flags, scales, section)
    code = spread(codes[...].astype(F32), 0).astype(jnp.int32)
    row = lax.broadcasted_iota(jnp.int32, (ROWS, LANES), 0)
    lane = lane_of()
    at_x = jnp.zeros((ROWS, LANES), jnp.int32) + lax.axis_index("gx")
    at_y = jnp.zeros((ROWS, LANES), jnp.int32) + lax.axis_index("gy")
    both = jnp.logical_and
    ends = (
        (both(at_x == 0, row < 8), both(at_x == columns - 1, row >= 8)),
        (at_y == 0, at_y == lines - 1),
        (both(row % 8 == 0, lane < 64), both(row % 8 == 7, lane >= 64)),
    )
    for d in range(3):
        index = node_index(d)
        low = (1 - 2 * ((code >> (2 * d)) & 1)).astype(F32)
        high = (1 - 2 * ((code >> (2 * d + 1)) & 1)).astype(F32)
        wall = jnp.where(both(ends[d][0], index == 0), low, 0.0)
        walls[d] = jnp.where(both(ends[d][1], index == 3), high, wall)


def volume_kernel(mix, coupling, state, start, walls, table, out, near, high, low, total):
    from_start, from_here = mix
    gas = Gas(lambda v: state[v], (0, 1, 2))
    for var in range(VARS):
        value = state[var]
        for d in range(3):
            flux = value * gas.velocity[d]
            if var == SPECIES + d:
                flux = flux + gas.pressure
            if var == ENERGY:
                flux = flux + gas.pressure * gas.velocity[d]
            at = pl.ds(LANES * d, LANES)
            high[block(var), at], low[block(var), at] = split(flux)
    total[...] = product(high[...], low[...], table)
    face = Face(walls[2], 2)
    for var in range(VARS):
        value = state[var]
        near[var] = face.outside(var, value, *shift_z(value))
    gain = face_gain(face, 2, gas, Gas(lambda v: near[v], (2,)))
    for var in range(VARS):
        value = state[var]
        change = gain(var, value, near[var]) - total[block(var), :]
        if var < SPECIES:
            for other in range(SPECIES):
                change = change + coupling[var, other] * state[other]
        here = from_here * value + (from_here * STEP) * change
        if from_start:
            here = here + from_start * start[var]
        out[var] = here


def fetch_near(state, walls, received, near_x, near_y):
    face_x, face_y = Face(walls[0], 0), Face(walls[1], 1)
    for var in range(VARS):
        value = state[var]
        near_x[var] = face_x.outside(var, value, *received.along_x(var, value))
        near_y[var] = face_y.outside(var, value, *received.along_y(var))


def face_kernel(section, share, last, state, inner, walls, factors, mean, *refs):
    if last:
        near_x, near_y, out, high, low = refs
    else:
        xa, xb, ya, yb, out, near_x, near_y, sa, sb, sc, sd, high, low = refs
        fetch_near(state, walls, Received((xa, xb, ya, yb)), near_x, near_y)
    gas = Gas(lambda v: state[v], (0, 1))
    gain_x = face_gain(Face(walls[0], 0), 0, gas, Gas(lambda v: near_x[v], (0,)))
    gain_y = face_gain(Face(walls[1], 1), 1, gas, Gas(lambda v: near_y[v], (1,)))
    for var in range(VARS):
        value = state[var]
        change = gain_x(var, value, near_x[var]) + gain_y(var, value, near_y[var])
        out[var] = inner[var] + (share * STEP) * change
    get = limited(lambda v: out[v], factors[section], high, low, mean, False)
    for var in range(VARS):
        out[var] = get(var)
    if not last:
        pack(lambda v: out[v], (sa, sb, sc, sd))


def back_volume_kernel(coupling, state, lam, near, walls, table, out, high, low, total):
    for var in range(VARS):
        high[block(var), :], low[block(var), :] = split(lam[var])
    total[...] = product(high[...], low[...], table)
    gas = Gas(lambda v: state[v], (0, 1, 2))
    other = Gas(lambda v: near[v], (2,))
    face = Face(walls[2], 2)
    speeds = gas.speed[2] + other.speed[2]
    back = Back(gas)
    for var in range(VARS):
        value, own = state[var], lam[var]
        outside = face.outside(var, own, *shift_z(own))
        part = back.flux(var, 0, value, -total[block(var), pl.ds(0, LANES)])
        part = part + back.flux(var, 1, value, -total[block(var), pl.ds(LANES, LANES)])
        part = part + back.flux(
            var, 2, value, -total[block(var), pl.ds(2 * LANES, LANES)] - face.three * (own + outside)
        )
        jump = face.half * (outside - own)
        back.wave(2, jump * (value - near[var]))
        out[var] = part + speeds * jump
    back.close()
    for var in range(VARS):
        change = out[var] + back.rest(var)
        if var < SPECIES:
            for other_var in range(SPECIES):
                change = change + coupling[other_var, var] * lam[other_var]
        out[var] = lam[var] + STEP * change


def back_faces(state, lam, near_x, near_y, walls, received, inner, out):
    gas = Gas(lambda v: state[v], (0, 1))
    faces = (Face(walls[0], 0), Face(walls[1], 1))
    nears = (near_x, near_y)
    speeds = [gas.speed[d] + Gas(lambda v, d=d: nears[d][v], (d,)).speed[d] for d in range(2)]
    back = Back(gas)
    for var in range(VARS):
        value, own = state[var], lam[var]
        part = inner[var]
        for d in range(2):
            sides = received.along_x(var, own) if d == 0 else received.along_y(var)
            outside = faces[d].outside(var, own, *sides)
            part = part + STEP * back.flux(var, d, value, -faces[d].three * (own + outside))
            jump = faces[d].half * (outside - own)
            back.wave(d, jump * (value - nears[d][var]))
            part = part + STEP * (speeds[d] * jump)
        out[var] = part
    back.close()
    for var in range(VARS):
        out[var] = out[var] + STEP * back.rest(var)


def turn_kernel(state, lam, inner, walls, factors, mean_t, *refs):
    qa, qb, qc, qd, la, lb, lc, ld = refs[:8]
    below, carry, near_x, near_y, sa, sb, sc, sd, high, low, work = refs[8:]
    fetch_near(state, walls, Received((qa, qb, qc, qd)), near_x, near_y)
    back_faces(state, lam, near_x, near_y, walls, Received((la, lb, lc, ld), 1), inner, work)
    get = limited(lambda v: work[v], factors[1], high, low, mean_t, True)
    for var in range(VARS):
        reverse = get(var)
        carry[var] = 0.5 * lam[var] + 0.75 * reverse
        below[var] = 0.25 * reverse
    pack(lambda v: below[v], (sa, sb, sc, sd))


def middle_kernel(state, lam, inner, near_x, near_y, walls, factors, mean_t, *refs):
    la, lb, lc, ld, below, sa, sb, sc, sd, high, low, work = refs
    back_faces(state, lam, near_x, near_y, walls, Received((la, lb, lc, ld)), inner, work)
    get = limited(lambda v: work[v], factors[0], high, low, mean_t, True)
    for var in range(VARS):
        below[var] = get(var)
    pack(lambda v: below[v], (sa, sb, sc, sd))


def end_kernel(state, lam, inner, near_x, near_y, carry, walls, la, lb, lc, ld, out):
    back_faces(state, lam, near_x, near_y, walls, Received((la, lb, lc, ld)), inner, out)
    for var in range(VARS):
        out[var] = out[var] + carry[var]


FIELD = (VARS, ROWS, LANES)
TABLE = (3, ROWS, LANES)


def call(kernel, inputs, outputs, scratch=(), scalars=0):
    specs = [
        pl.BlockSpec(memory_space=pltpu.SMEM if at < scalars else pltpu.VMEM) for at in range(len(inputs))
    ]
    return pl.pallas_call(
        kernel,
        in_specs=specs,
        out_specs=[pl.BlockSpec(memory_space=pltpu.VMEM)] * len(outputs),
        out_shape=[jax.ShapeDtypeStruct(shape, F32) for shape in outputs],
        scratch_shapes=list(scratch),
        compiler_params=pltpu.CompilerParams(vmem_limit_bytes=8 << 20),
    )(*inputs)


def packs(parts):
    return [(parts * GROUPS, 8, LANES)] * 2 + [(parts * GROUPS, ROWS, LANES)] * 2


def halved(width):
    return [pltpu.VMEM((VARS * ROWS, width), BF16)] * 2


def exchange(sent):
    def swap(values, axis, first):
        count = lax.axis_size(axis)
        moves = []
        for low in range(first, count + first, 2):
            a, b = low % count, (low + 1) % count
            moves += [(a, b), (b, a)]
        return lax.ppermute(values, axis, moves)

    xa, xb, ya, yb = sent
    yb = swap(yb, "gy", 1)
    xb = swap(xb, "gx", 1)
    ya = swap(ya, "gy", 0)
    xa = swap(xa, "gx", 0)
    return [xa, xb, ya, yb]


def per_device(state_start, adjoint_end, limiter_flags, limiter_scales, face_codes, reaction_rates):
    forward, backward, mean, mean_t = [halves(table) for table in node_tables()]
    q0 = state_start.reshape(FIELD)
    adjoint = adjoint_end.reshape(FIELD)
    flags = limiter_flags.reshape(6, 16)
    scales = limiter_scales.reshape(6, 16)
    codes = face_codes.reshape(2, 16)
    off_diag = reaction_rates * (1.0 - jnp.eye(SPECIES, dtype=F32))
    coupling = off_diag - jnp.diag(jnp.sum(off_diag, axis=0))
    narrow, wide = halved(LANES), halved(3 * LANES)
    total = [pltpu.VMEM((VARS * ROWS, LANES), F32)]
    total3 = [pltpu.VMEM((VARS * ROWS, 3 * LANES), F32)]
    work = [pltpu.VMEM(FIELD, F32)]

    lam3, *sent = call(start_kernel, [q0, adjoint, flags, scales, mean_t], [FIELD] + packs(2), narrow)
    got0 = exchange(sent)
    size = functools.partial(table_kernel, lax.axis_size("gx"), lax.axis_size("gy"))
    walls, factors = call(size, [codes, flags, scales], [TABLE, TABLE])

    def inner(mix, state):
        kernel = functools.partial(volume_kernel, mix)
        return call(kernel, [coupling, state, q0, walls, forward], [FIELD, FIELD], wide + total, 1)

    def back_inner(state, lam, near):
        return call(
            back_volume_kernel, [coupling, state, lam, near, walls, backward], [FIELD], narrow + total3, 1
        )[0]

    def outer(section, share, state, part, got):
        kernel = functools.partial(face_kernel, section, share, False)
        out, near_x, near_y, *sent = call(
            kernel, [state, part, walls, factors, mean, *got], [FIELD] * 3 + packs(1), narrow
        )
        return out, near_x, near_y, sent

    part, z0 = inner((0.0, 1.0), q0)
    q1, x0, y0, sent = outer(0, 1.0, q0, part, got0)
    got1 = exchange(sent)
    part, z1 = inner((0.75, 0.25), q1)
    q2, x1, y1, sent = outer(1, 0.25, q1, part, got1)
    got2 = exchange(sent)
    part, z2 = inner((1.0 / 3.0, 2.0 / 3.0), q2)
    back = back_inner(q2, lam3, z2)
    lam2, carry, x2, y2, *sent = call(
        turn_kernel,
        [q2, lam3, back, walls, factors, mean_t, *got2, *got0],
        [FIELD] * 4 + packs(1),
        narrow + work,
    )
    got = exchange(sent)
    last = functools.partial(face_kernel, 2, 2.0 / 3.0, True)
    state_end = call(last, [q2, part, walls, factors, mean, x2, y2], [FIELD], narrow)[0]
    back = back_inner(q1, lam2, z1)
    lam1, *sent = call(
        middle_kernel,
        [q1, lam2, back, x1, y1, walls, factors, mean_t, *got],
        [FIELD] + packs(1),
        narrow + work,
    )
    got = exchange(sent)
    back = back_inner(q0, lam1, z0)
    adjoint_start = call(end_kernel, [q0, lam1, back, x0, y0, carry, walls, *got], [FIELD])[0]
    return state_end.reshape(state_start.shape), adjoint_start.reshape(state_start.shape)


def solution(mesh):
    field = P(None, "gx", "gy", None)
    return jax.shard_map(
        per_device,
        mesh=mesh,
        in_specs=(field, field, field, field, P("gx", "gy", None), P()),
        out_specs=(field, field),
        check_vma=False,
    )
```

```python
import functools

import jax
import jax.numpy as jnp
import numpy as np
from jax import lax
from jax.experimental import pallas as pl
from jax.experimental.pallas import tpu as pltpu
from jax.sharding import PartitionSpec as P

SPECIES = 21
VARS = 25
ENERGY = 24
GROUPS = 7
STEP = 0.008
F32 = jnp.float32
BF16 = jnp.bfloat16
ROWS = 16
LANES = 128


def node_tables():
    points = np.array([-1.0, -1.0 / np.sqrt(5.0), 1.0 / np.sqrt(5.0), 1.0])
    weights = np.array([1.0, 5.0, 5.0, 1.0]) / 6.0
    bary = np.array([1.0 / np.prod([points[a] - points[b] for b in range(4) if b != a]) for a in range(4)])
    deriv = np.zeros((4, 4))
    for a in range(4):
        for b in range(4):
            if a != b:
                deriv[a, b] = bary[b] / bary[a] / (points[a] - points[b])
        deriv[a, a] = -np.sum(deriv[a])
    eye = np.eye(4)
    pair = np.eye(2)
    ops = [
        np.kron(np.kron(deriv.T, eye), eye),
        np.kron(np.kron(eye, deriv.T), eye),
        np.kron(np.kron(eye, eye), deriv.T),
    ]
    grads = [np.kron(pair, op) for op in ops]
    cube = np.kron(np.kron(weights, weights), weights) / 8.0
    mean = np.kron(pair, np.repeat(cube[:, None], 64, axis=1))
    forward = np.concatenate(grads, axis=0)
    backward = np.concatenate([g.T for g in grads], axis=1)
    return forward, backward, mean, mean.T


def halves(table):
    table = np.asarray(table, np.float32)
    high = table.astype(jnp.bfloat16)
    low = (table - high.astype(np.float32)).astype(jnp.bfloat16)
    return jnp.asarray(np.stack([high, low]))


def split(values):
    high = values.astype(BF16)
    return high, (values - high.astype(F32)).astype(BF16)


def product(high, low, table):
    dot = functools.partial(jnp.dot, preferred_element_type=F32)
    return dot(high, table[0]) + dot(high, table[1]) + dot(low, table[0])


def roll(values, shift, axis):
    shift = shift % values.shape[axis]
    return values if shift == 0 else pltpu.roll(values, shift, axis)


def lane_of(rows=ROWS):
    return lax.broadcasted_iota(jnp.int32, (rows, LANES), 1)


def node_index(direction, rows=ROWS):
    return (lane_of(rows) >> (4, 2, 0)[direction]) & 3


def block(var):
    return pl.ds(ROWS * var, ROWS)


class Face:
    def __init__(self, wall, direction):
        index = node_index(direction)
        inside = wall == 0.0
        self.low = jnp.logical_and(index == 0, inside)
        self.high = jnp.logical_and(index == 3, inside)
        self.sign = jnp.where(wall < 0.0, -1.0, 1.0)
        live = jnp.where(wall > 0.0, 0.0, 1.0)
        self.three = jnp.where(index == 0, 3.0, jnp.where(index == 3, -3.0, 0.0)) * live
        self.half = jnp.where(jnp.logical_or(index == 0, index == 3), 1.5, 0.0) * live
        self.momentum = SPECIES + direction

    def outside(self, var, own, low, high):
        edge = own * self.sign if var == self.momentum else own
        return jnp.where(self.low, low, jnp.where(self.high, high, edge))


def shift_z(values):
    first = lane_of() < 64
    low = roll(values, 61, 1)
    low = jnp.where(first, roll(low, 1, 0), low)
    high = roll(values, 67, 1)
    high = jnp.where(first, high, roll(high, ROWS - 1, 0))
    return low, high


class Received:
    def __init__(self, refs, part=0):
        even_x = (jnp.zeros((8, LANES), jnp.int32) + lax.axis_index("gx") % 2) == 0
        even_y = (jnp.zeros((ROWS, LANES), jnp.int32) + lax.axis_index("gy") % 2) == 0
        yb, xb, ya, xa = refs
        self.packs = []
        for group in range(GROUPS):
            at = part * GROUPS + group
            a, b, c, d = xa[at], xb[at], ya[at], yb[at]
            self.packs.append(
                (
                    jnp.where(even_x, b, a),
                    jnp.where(even_x, a, b),
                    jnp.where(even_y, d, c),
                    jnp.where(even_y, c, d),
                )
            )

    def along_x(self, var, own):
        group, slot = divmod(var, 4)
        low, high = self.packs[group][:2]
        first, second = own[:8], own[8:]
        return (
            jnp.concatenate([roll(low, -16 * slot, 1), roll(first, -48, 1)], axis=0),
            jnp.concatenate([roll(second, 48, 1), roll(high, 16 * (3 - slot), 1)], axis=0),
        )

    def along_y(self, var):
        group, slot = divmod(var, 4)
        low, high = self.packs[group][2:]
        return roll(low, -4 * slot, 1), roll(high, 4 * (3 - slot), 1)


def pack(field, refs, part=0):
    even_x = (jnp.zeros((8, LANES), jnp.int32) + lax.axis_index("gx") % 2) == 0
    even_y = (jnp.zeros((ROWS, LANES), jnp.int32) + lax.axis_index("gy") % 2) == 0
    yb, xb, ya, xa = refs
    spot_x, spot_y = node_index(0, 8), node_index(1)

    def merged(spot, pieces):
        out = pieces[3]
        for slot in (2, 1, 0):
            out = jnp.where(spot == slot, pieces[slot], out)
        return out

    for group in range(GROUPS):
        at = part * GROUPS + group
        own = [field(min(4 * group + slot, ENERGY)) for slot in range(4)]
        if group == GROUPS - 1:
            x_low, x_high = own[0][:8], roll(own[0][8:], -48, 1)
            y_low, y_high = own[0], roll(own[0], -12, 1)
        else:
            x_low = merged(spot_x, [roll(own[s][:8], 16 * s, 1) for s in range(4)])
            x_high = merged(spot_x, [roll(own[s][8:], 16 * (s - 3), 1) for s in range(4)])
            y_low = merged(spot_y, [roll(own[s], 4 * s, 1) for s in range(4)])
            y_high = merged(spot_y, [roll(own[s], 4 * (s - 3), 1) for s in range(4)])
        xa[at] = jnp.where(even_x, x_high, x_low)
        xb[at] = jnp.where(even_x, x_low, x_high)
        ya[at] = jnp.where(even_y, y_high, y_low)
        yb[at] = jnp.where(even_y, y_low, y_high)


class Gas:
    def __init__(self, field, directions):
        density = field(0)
        for var in range(1, SPECIES):
            density = density + field(var)
        self.inverse = 1.0 / density
        self.momenta = [field(SPECIES + e) for e in range(3)]
        m0, m1, m2 = self.momenta
        self.square = m0 * m0 + m1 * m1 + m2 * m2
        self.pressure = 0.4 * (field(ENERGY) - 0.5 * self.square * self.inverse)
        self.velocity = {d: self.momenta[d] * self.inverse for d in directions}
        sound = 1.4 * self.pressure * self.inverse
        self.speed = {d: jnp.sqrt(self.velocity[d] * self.velocity[d] + sound) for d in directions}


def face_gain(face, direction, own, other):
    weight = face.half * (own.speed[direction] + other.speed[direction])
    u_in, u_out = own.velocity[direction], other.velocity[direction]
    take, leave = face.three * u_out + weight, face.three * u_in + weight

    def gain(var, inside, outside):
        total = outside * take - inside * leave
        if var == face.momentum:
            total = total + face.three * (other.pressure - own.pressure)
        if var == ENERGY:
            total = total + face.three * (other.pressure * u_out - own.pressure * u_in)
        return total

    return gain


class Back:
    def __init__(self, gas):
        self.gas = gas
        zero = jnp.zeros((ROWS, LANES), F32)
        self.speed = {}
        self.velocity = {}
        self.pressure = zero

    def flux(self, var, direction, value, cotangent):
        gas = self.gas
        term = cotangent * value
        if var == ENERGY:
            term = term + cotangent * gas.pressure
            self.pressure = self.pressure + cotangent * gas.velocity[direction]
        if var == SPECIES + direction:
            self.pressure = self.pressure + cotangent
        held = self.velocity.get(direction)
        self.velocity[direction] = term if held is None else held + term
        return cotangent * gas.velocity[direction]

    def wave(self, direction, term):
        held = self.speed.get(direction)
        self.speed[direction] = term if held is None else held + term

    def close(self):
        gas = self.gas
        inverse, pressure = gas.inverse, self.pressure
        into = jnp.zeros((ROWS, LANES), F32)
        for direction, term in self.speed.items():
            scaled = term / gas.speed[direction]
            self.velocity[direction] = self.velocity[direction] + scaled * gas.velocity[direction]
            pressure = pressure + 0.7 * scaled * inverse
            into = into + 0.7 * scaled * gas.pressure
        for direction, term in self.velocity.items():
            into = into + term * gas.momenta[direction]
        into = into - 0.2 * pressure * gas.square
        self.species = -inverse * inverse * into
        self.momentum = []
        for e in range(3):
            term = -0.4 * pressure * gas.momenta[e]
            if e in self.velocity:
                term = term + self.velocity[e]
            self.momentum.append(term * inverse)
        self.energy = 0.4 * pressure

    def rest(self, var):
        if var < SPECIES:
            return self.species
        return self.energy if var == ENERGY else self.momentum[var - SPECIES]


def spread(lines):
    place = lax.broadcasted_iota(jnp.int32, (8, 16), 0)
    element = lax.broadcasted_iota(jnp.int32, (8, 16), 1)
    left = lane_of(8) < 64
    columns = []
    for column in range(2):
        line = jnp.broadcast_to(lines[column], (8, 16))
        picked = [
            jnp.sum(jnp.where(element == 2 * place + half, line, 0.0), axis=1, keepdims=True)
            for half in range(2)
        ]
        columns.append(jnp.where(left, picked[0], picked[1]))
    return jnp.concatenate(columns, axis=0)


def spread_rate(coupling, source, target):
    return jnp.broadcast_to(coupling[source, target : target + 1, :], (ROWS, LANES))


def damping(flags, scales, section):
    lines = []
    for column in range(2):
        at = (section, column)
        lines.append(jnp.where(flags[at] == 1, scales[at], 1.0))
    return spread(lines)


def limited(field, factor, high, low, table, transposed):
    for var in range(VARS):
        value = field(var)
        if transposed:
            value = (1.0 - factor) * value
        high[block(var), :], low[block(var), :] = split(value)
    means = product(high[...], low[...], table)

    def get(var):
        mean = means[ROWS * var : ROWS * (var + 1)]
        if transposed:
            return factor * field(var) + mean
        return mean + factor * (field(var) - mean)

    return get


def start_kernel(count, *refs):
    there, here, sent, arrived = refs[:count], refs[count : 2 * count], refs[2 * count : -1], refs[-1]
    copies = [pltpu.make_async_copy(there[k], here[k], arrived.at[k]) for k in range(count)]
    for copy in copies:
        copy.start()
    copies[0].wait()
    pack(lambda v: here[0][v], sent)
    for copy in copies[1:]:
        copy.wait()


def setup_kernel(columns, lines, adjoint, rates, codes, flags, scales, mean_t, lam, yb, xb, ya, xa, walls, factors, coupling, high, low):
    row = lax.broadcasted_iota(jnp.int32, (SPECIES, SPECIES), 0)
    same = row == lax.broadcasted_iota(jnp.int32, (SPECIES, SPECIES), 1)
    off_diag = jnp.where(same, 0.0, rates[...])
    leaving = jnp.sum(off_diag, axis=0, keepdims=True)
    full = jnp.where(same, -jnp.broadcast_to(leaving, (SPECIES, SPECIES)), off_diag)
    for source in range(SPECIES):
        coupling[source] = jnp.broadcast_to(full[:, source : source + 1], (SPECIES, LANES))
    for section in range(3):
        factors[section] = damping(flags, scales, section)
    get = limited(lambda v: adjoint[v], factors[2], high, low, mean_t, True)
    for var in range(VARS):
        lam[var] = (2.0 / 3.0) * get(var)
    pack(lambda v: lam[v], (yb, xb, ya, xa))
    code = spread([codes[column].astype(F32) for column in range(2)]).astype(jnp.int32)
    row = lax.broadcasted_iota(jnp.int32, (ROWS, LANES), 0)
    lane = lane_of()
    at_x = jnp.zeros((ROWS, LANES), jnp.int32) + lax.axis_index("gx")
    at_y = jnp.zeros((ROWS, LANES), jnp.int32) + lax.axis_index("gy")
    both = jnp.logical_and
    ends = (
        (both(at_x == 0, row < 8), both(at_x == columns - 1, row >= 8)),
        (at_y == 0, at_y == lines - 1),
        (both(row % 8 == 0, lane < 64), both(row % 8 == 7, lane >= 64)),
    )
    for d in range(3):
        index = node_index(d)
        low = (1 - 2 * ((code >> (2 * d)) & 1)).astype(F32)
        high = (1 - 2 * ((code >> (2 * d + 1)) & 1)).astype(F32)
        wall = jnp.where(both(ends[d][0], index == 0), low, 0.0)
        walls[d] = jnp.where(both(ends[d][1], index == 3), high, wall)


def volume_kernel(mix, coupling, state, start, walls, table, out, near, high, low, total):
    from_start, from_here = mix
    gas = Gas(lambda v: state[v], (0, 1, 2))
    for var in range(VARS):
        value = state[var]
        for d in range(3):
            flux = value * gas.velocity[d]
            if var == SPECIES + d:
                flux = flux + gas.pressure
            if var == ENERGY:
                flux = flux + gas.pressure * gas.velocity[d]
            at = pl.ds(LANES * d, LANES)
            high[block(var), at], low[block(var), at] = split(flux)
    total[...] = product(high[...], low[...], table)
    face = Face(walls[2], 2)
    for var in range(VARS):
        value = state[var]
        near[var] = face.outside(var, value, *shift_z(value))
    gain = face_gain(face, 2, gas, Gas(lambda v: near[v], (2,)))
    for var in range(VARS):
        value = state[var]
        change = gain(var, value, near[var]) - total[block(var), :]
        if var < SPECIES:
            for other in range(SPECIES):
                change = change + spread_rate(coupling, other, var) * state[other]
        here = from_here * value + (from_here * STEP) * change
        if from_start:
            here = here + from_start * start[var]
        out[var] = here


def fetch_near(state, walls, received, near_x, near_y):
    face_x, face_y = Face(walls[0], 0), Face(walls[1], 1)
    for var in range(VARS):
        value = state[var]
        near_x[var] = face_x.outside(var, value, *received.along_x(var, value))
        near_y[var] = face_y.outside(var, value, *received.along_y(var))


def face_kernel(section, share, last, state, inner, walls, factors, mean, *refs):
    along = ()
    if last:
        near_x, near_y, out, high, low = refs
    else:
        along = refs[4:-9]
        xa, xb, ya, yb = refs[:4]
        out, near_x, near_y, sa, sb, sc, sd, high, low = refs[-9:]
        fetch_near(state, walls, Received((xa, xb, ya, yb)), near_x, near_y)
    gas = Gas(lambda v: state[v], (0, 1))
    gain_x = face_gain(Face(walls[0], 0), 0, gas, Gas(lambda v: near_x[v], (0,)))
    gain_y = face_gain(Face(walls[1], 1), 1, gas, Gas(lambda v: near_y[v], (1,)))
    for var in range(VARS):
        value = state[var]
        change = gain_x(var, value, near_x[var]) + gain_y(var, value, near_y[var])
        out[var] = inner[var] + (share * STEP) * change
    get = limited(lambda v: out[v], factors[section], high, low, mean, False)
    for var in range(VARS):
        out[var] = get(var)
    if not last:
        pack(lambda v: out[v], (sa, sb, sc, sd))
        for held, sent in zip(along, (sa, sb, sc, sd)):
            sent[GROUPS:] = held[...]


def back_volume_kernel(coupling, state, lam, near, walls, table, out, high, low, total):
    for var in range(VARS):
        high[block(var), :], low[block(var), :] = split(lam[var])
    total[...] = product(high[...], low[...], table)
    gas = Gas(lambda v: state[v], (0, 1, 2))
    other = Gas(lambda v: near[v], (2,))
    face = Face(walls[2], 2)
    speeds = gas.speed[2] + other.speed[2]
    back = Back(gas)
    for var in range(VARS):
        value, own = state[var], lam[var]
        outside = face.outside(var, own, *shift_z(own))
        part = back.flux(var, 0, value, -total[block(var), pl.ds(0, LANES)])
        part = part + back.flux(var, 1, value, -total[block(var), pl.ds(LANES, LANES)])
        part = part + back.flux(
            var, 2, value, -total[block(var), pl.ds(2 * LANES, LANES)] - face.three * (own + outside)
        )
        jump = face.half * (outside - own)
        back.wave(2, jump * (value - near[var]))
        out[var] = part + speeds * jump
    back.close()
    for var in range(VARS):
        change = out[var] + back.rest(var)
        if var < SPECIES:
            for other_var in range(SPECIES):
                change = change + spread_rate(coupling, var, other_var) * lam[other_var]
        out[var] = lam[var] + STEP * change


def back_faces(state, lam, near_x, near_y, walls, received, inner, out):
    gas = Gas(lambda v: state[v], (0, 1))
    faces = (Face(walls[0], 0), Face(walls[1], 1))
    nears = (near_x, near_y)
    speeds = [gas.speed[d] + Gas(lambda v, d=d: nears[d][v], (d,)).speed[d] for d in range(2)]
    back = Back(gas)
    for var in range(VARS):
        value, own = state[var], lam[var]
        part = inner[var]
        for d in range(2):
            sides = received.along_x(var, own) if d == 0 else received.along_y(var)
            outside = faces[d].outside(var, own, *sides)
            part = part + STEP * back.flux(var, d, value, -faces[d].three * (own + outside))
            jump = faces[d].half * (outside - own)
            back.wave(d, jump * (value - nears[d][var]))
            part = part + STEP * (speeds[d] * jump)
        out[var] = part
    back.close()
    for var in range(VARS):
        out[var] = out[var] + STEP * back.rest(var)


def turn_kernel(state, lam, inner, walls, factors, mean_t, *refs):
    got = refs[:4]
    below, carry, near_x, near_y, sa, sb, sc, sd, high, low, work = refs[4:]
    fetch_near(state, walls, Received(got), near_x, near_y)
    back_faces(state, lam, near_x, near_y, walls, Received(got, 1), inner, work)
    get = limited(lambda v: work[v], factors[1], high, low, mean_t, True)
    for var in range(VARS):
        reverse = get(var)
        carry[var] = 0.5 * lam[var] + 0.75 * reverse
        below[var] = 0.25 * reverse
    pack(lambda v: below[v], (sa, sb, sc, sd))


def middle_kernel(state, lam, inner, near_x, near_y, walls, factors, mean_t, *refs):
    la, lb, lc, ld, below, sa, sb, sc, sd, high, low, work = refs
    back_faces(state, lam, near_x, near_y, walls, Received((la, lb, lc, ld)), inner, work)
    get = limited(lambda v: work[v], factors[0], high, low, mean_t, True)
    for var in range(VARS):
        below[var] = get(var)
    pack(lambda v: below[v], (sa, sb, sc, sd))


def end_kernel(state, lam, inner, near_x, near_y, carry, walls, la, lb, lc, ld, out):
    back_faces(state, lam, near_x, near_y, walls, Received((la, lb, lc, ld)), inner, out)
    for var in range(VARS):
        out[var] = out[var] + carry[var]


FIELD = (VARS, ROWS, LANES)
TABLE = (3, ROWS, LANES)


def call(kernel, inputs, outputs, scratch=()):
    return pl.pallas_call(
        kernel,
        in_specs=[pl.BlockSpec(memory_space=pltpu.VMEM)] * len(inputs),
        out_specs=[pl.BlockSpec(memory_space=pltpu.VMEM)] * len(outputs),
        out_shape=[jax.ShapeDtypeStruct(shape, F32) for shape in outputs],
        scratch_shapes=list(scratch),
        compiler_params=pltpu.CompilerParams(vmem_limit_bytes=8 << 20),
        name=getattr(kernel, "func", kernel).__name__,
    )(*inputs)


def packs(parts):
    return [(parts * GROUPS, ROWS, LANES), (parts * GROUPS, 8, LANES), (parts * GROUPS, ROWS, LANES), (parts * GROUPS, 8, LANES)]


def halved(width):
    return [pltpu.VMEM((VARS * ROWS, width), BF16)] * 2


def exchange(sent):
    def swap(values, axis, first):
        count = lax.axis_size(axis)
        moves = []
        for low in range(first, count + first, 2):
            a, b = low % count, (low + 1) % count
            moves += [(a, b), (b, a)]
        return lax.ppermute(values, axis, moves)

    yb, xb, ya, xa = sent
    yb = swap(yb, "gy", 1)
    xb = swap(xb, "gx", 1)
    ya = swap(ya, "gy", 0)
    xa = swap(xa, "gx", 0)
    return [yb, xb, ya, xa]


def per_device(state_start, adjoint_end, limiter_flags, limiter_scales, face_codes, reaction_rates):
    forward, backward, mean, mean_t = [halves(table) for table in node_tables()]
    q0 = state_start.reshape(FIELD)
    adjoint = adjoint_end.reshape(FIELD)
    narrow, wide = halved(LANES), halved(3 * LANES)
    total = [pltpu.VMEM((VARS * ROWS, LANES), F32)]
    total3 = [pltpu.VMEM((VARS * ROWS, 3 * LANES), F32)]
    work = [pltpu.VMEM(FIELD, F32)]

    held = [q0, adjoint, reaction_rates, face_codes, limiter_flags, limiter_scales]
    held += [mean_t, forward, mean, backward]
    got = pl.pallas_call(
        functools.partial(start_kernel, len(held)),
        in_specs=[pl.BlockSpec(memory_space=pltpu.HBM)] * len(held),
        out_specs=[pl.BlockSpec(memory_space=pltpu.VMEM)] * (len(held) + 4),
        out_shape=[jax.ShapeDtypeStruct(v.shape, v.dtype) for v in held]
        + [jax.ShapeDtypeStruct(shape, F32) for shape in packs(1)],
        scratch_shapes=[pltpu.SemaphoreType.DMA((len(held),))],
        compiler_params=pltpu.CompilerParams(vmem_limit_bytes=8 << 20),
        name="start_kernel",
    )(*[pltpu.with_memory_space_constraint(v, pltpu.HBM) for v in held])
    q0, adjoint, rates, codes, flags, scales, mean_t, forward, mean, backward = got[: len(held)]
    got = exchange(got[len(held) :])
    size = functools.partial(setup_kernel, lax.axis_size("gx"), lax.axis_size("gy"))
    lam3, *along, walls, factors, coupling = call(
        size,
        [adjoint, rates, codes, flags, scales, mean_t],
        [FIELD] + packs(1) + [TABLE, TABLE, (SPECIES, SPECIES, LANES)],
        narrow,
    )

    def inner(mix, state):
        kernel = functools.partial(volume_kernel, mix)
        return call(kernel, [coupling, state, q0, walls, forward], [FIELD, FIELD], wide + total)

    def back_inner(state, lam, near):
        return call(
            back_volume_kernel, [coupling, state, lam, near, walls, backward], [FIELD], narrow + total3
        )[0]

    def outer(section, share, state, part, got, along=()):
        kernel = functools.partial(face_kernel, section, share, False)
        out, near_x, near_y, *sent = call(
            kernel, [state, part, walls, factors, mean, *got, *along],
            [FIELD] * 3 + packs(2 if along else 1),
            narrow,
        )
        return out, near_x, near_y, sent

    part, z0 = inner((0.0, 1.0), q0)
    q1, x0, y0, sent = outer(0, 1.0, q0, part, got)
    got = exchange(sent)
    part, z1 = inner((0.75, 0.25), q1)
    q2, x1, y1, sent = outer(1, 0.25, q1, part, got, along)
    got = exchange(sent)
    part, z2 = inner((1.0 / 3.0, 2.0 / 3.0), q2)
    back = back_inner(q2, lam3, z2)
    lam2, carry, x2, y2, *sent = call(
        turn_kernel,
        [q2, lam3, back, walls, factors, mean_t, *got],
        [FIELD] * 4 + packs(1),
        narrow + work,
    )
    got = exchange(sent)
    last = functools.partial(face_kernel, 2, 2.0 / 3.0, True)
    state_end = call(last, [q2, part, walls, factors, mean, x2, y2], [FIELD], narrow)[0]
    back = back_inner(q1, lam2, z1)
    lam1, *sent = call(
        middle_kernel,
        [q1, lam2, back, x1, y1, walls, factors, mean_t, *got],
        [FIELD] + packs(1),
        narrow + work,
    )
    got = exchange(sent)
    back = back_inner(q0, lam1, z0)
    adjoint_start = call(end_kernel, [q0, lam1, back, x0, y0, carry, walls, *got], [FIELD])[0]
    return state_end.reshape(state_start.shape), adjoint_start.reshape(state_start.shape)


def solution(mesh):
    field = P(None, "gx", "gy", None)
    return jax.shard_map(
        per_device,
        mesh=mesh,
        in_specs=(field, field, field, field, P("gx", "gy", None), P()),
        out_specs=(field, field),
        check_vma=False,
    )
```

```python
import functools

import jax
import jax.numpy as jnp
import numpy as np
from jax import lax
from jax.experimental import pallas as pl
from jax.experimental.pallas import tpu as pltpu
from jax.sharding import PartitionSpec as P

SPECIES = 21
VARS = 25
ENERGY = 24
GROUPS = 7
STEP = 0.008
F32 = jnp.float32
BF16 = jnp.bfloat16
ROWS = 16
LANES = 128


def node_tables():
    points = np.array([-1.0, -1.0 / np.sqrt(5.0), 1.0 / np.sqrt(5.0), 1.0])
    weights = np.array([1.0, 5.0, 5.0, 1.0]) / 6.0
    bary = np.array([1.0 / np.prod([points[a] - points[b] for b in range(4) if b != a]) for a in range(4)])
    deriv = np.zeros((4, 4))
    for a in range(4):
        for b in range(4):
            if a != b:
                deriv[a, b] = bary[b] / bary[a] / (points[a] - points[b])
        deriv[a, a] = -np.sum(deriv[a])
    eye = np.eye(4)
    pair = np.eye(2)
    ops = [
        np.kron(np.kron(deriv.T, eye), eye),
        np.kron(np.kron(eye, deriv.T), eye),
        np.kron(np.kron(eye, eye), deriv.T),
    ]
    grads = [np.kron(pair, op) for op in ops]
    cube = np.kron(np.kron(weights, weights), weights) / 8.0
    mean = np.kron(pair, np.repeat(cube[:, None], 64, axis=1))
    forward = np.concatenate(grads, axis=0)
    backward = np.concatenate([g.T for g in grads], axis=1)
    return forward, backward, mean, mean.T


def halves(table):
    table = np.asarray(table, np.float32)
    high = table.astype(jnp.bfloat16)
    low = (table - high.astype(np.float32)).astype(jnp.bfloat16)
    return jnp.asarray(np.stack([high, low]))


def split(values):
    high = values.astype(BF16)
    return high, (values - high.astype(F32)).astype(BF16)


def product(high, low, table):
    dot = functools.partial(jnp.dot, preferred_element_type=F32)
    return dot(high, table[0]) + dot(high, table[1]) + dot(low, table[0])


def roll(values, shift, axis):
    shift = shift % values.shape[axis]
    return values if shift == 0 else pltpu.roll(values, shift, axis)


def lane_of(rows=ROWS):
    return lax.broadcasted_iota(jnp.int32, (rows, LANES), 1)


def node_index(direction, rows=ROWS):
    return (lane_of(rows) >> (4, 2, 0)[direction]) & 3


def block(var):
    return pl.ds(ROWS * var, ROWS)


class Face:
    def __init__(self, wall, direction):
        index = node_index(direction)
        inside = wall == 0.0
        self.low = jnp.logical_and(index == 0, inside)
        self.high = jnp.logical_and(index == 3, inside)
        self.sign = jnp.where(wall < 0.0, -1.0, 1.0)
        live = jnp.where(wall > 0.0, 0.0, 1.0)
        self.three = jnp.where(index == 0, 3.0, jnp.where(index == 3, -3.0, 0.0)) * live
        self.half = jnp.where(jnp.logical_or(index == 0, index == 3), 1.5, 0.0) * live
        self.momentum = SPECIES + direction

    def outside(self, var, own, low, high):
        edge = own * self.sign if var == self.momentum else own
        return jnp.where(self.low, low, jnp.where(self.high, high, edge))


def shift_z(values):
    first = lane_of() < 64
    low = roll(values, 61, 1)
    low = jnp.where(first, roll(low, 1, 0), low)
    high = roll(values, 67, 1)
    high = jnp.where(first, high, roll(high, ROWS - 1, 0))
    return low, high


class Received:
    def __init__(self, refs, part=0):
        even_x = (jnp.zeros((8, LANES), jnp.int32) + lax.axis_index("gx") % 2) == 0
        even_y = (jnp.zeros((ROWS, LANES), jnp.int32) + lax.axis_index("gy") % 2) == 0
        yb, xb, ya, xa = refs
        self.packs = []
        for group in range(GROUPS):
            at = part * GROUPS + group
            a, b, c, d = xa[at], xb[at], ya[at], yb[at]
            self.packs.append(
                (
                    jnp.where(even_x, b, a),
                    jnp.where(even_x, a, b),
                    jnp.where(even_y, d, c),
                    jnp.where(even_y, c, d),
                )
            )

    def along_x(self, var, own):
        group, slot = divmod(var, 4)
        low, high = self.packs[group][:2]
        first, second = own[:8], own[8:]
        return (
            jnp.concatenate([roll(low, -16 * slot, 1), roll(first, -48, 1)], axis=0),
            jnp.concatenate([roll(second, 48, 1), roll(high, 16 * (3 - slot), 1)], axis=0),
        )

    def along_y(self, var):
        group, slot = divmod(var, 4)
        low, high = self.packs[group][2:]
        return roll(low, -4 * slot, 1), roll(high, 4 * (3 - slot), 1)


def pack(field, refs, part=0):
    even_x = (jnp.zeros((8, LANES), jnp.int32) + lax.axis_index("gx") % 2) == 0
    even_y = (jnp.zeros((ROWS, LANES), jnp.int32) + lax.axis_index("gy") % 2) == 0
    yb, xb, ya, xa = refs
    spot_x, spot_y = node_index(0, 8), node_index(1)

    def merged(spot, pieces):
        out = pieces[3]
        for slot in (2, 1, 0):
            out = jnp.where(spot == slot, pieces[slot], out)
        return out

    for group in range(GROUPS):
        at = part * GROUPS + group
        own = [field(min(4 * group + slot, ENERGY)) for slot in range(4)]
        if group == GROUPS - 1:
            x_low, x_high = own[0][:8], roll(own[0][8:], -48, 1)
            y_low, y_high = own[0], roll(own[0], -12, 1)
        else:
            x_low = merged(spot_x, [roll(own[s][:8], 16 * s, 1) for s in range(4)])
            x_high = merged(spot_x, [roll(own[s][8:], 16 * (s - 3), 1) for s in range(4)])
            y_low = merged(spot_y, [roll(own[s], 4 * s, 1) for s in range(4)])
            y_high = merged(spot_y, [roll(own[s], 4 * (s - 3), 1) for s in range(4)])
        xa[at] = jnp.where(even_x, x_high, x_low)
        xb[at] = jnp.where(even_x, x_low, x_high)
        ya[at] = jnp.where(even_y, y_high, y_low)
        yb[at] = jnp.where(even_y, y_low, y_high)


class Gas:
    def __init__(self, field, directions):
        density = field(0)
        for var in range(1, SPECIES):
            density = density + field(var)
        self.inverse = 1.0 / density
        self.momenta = [field(SPECIES + e) for e in range(3)]
        m0, m1, m2 = self.momenta
        self.square = m0 * m0 + m1 * m1 + m2 * m2
        self.pressure = 0.4 * (field(ENERGY) - 0.5 * self.square * self.inverse)
        self.velocity = {d: self.momenta[d] * self.inverse for d in directions}
        sound = 1.4 * self.pressure * self.inverse
        self.speed = {d: jnp.sqrt(self.velocity[d] * self.velocity[d] + sound) for d in directions}


def face_gain(face, direction, own, other):
    weight = face.half * (own.speed[direction] + other.speed[direction])
    u_in, u_out = own.velocity[direction], other.velocity[direction]
    take, leave = face.three * u_out + weight, face.three * u_in + weight

    def gain(var, inside, outside):
        total = outside * take - inside * leave
        if var == face.momentum:
            total = total + face.three * (other.pressure - own.pressure)
        if var == ENERGY:
            total = total + face.three * (other.pressure * u_out - own.pressure * u_in)
        return total

    return gain


class Back:
    def __init__(self, gas):
        self.gas = gas
        zero = jnp.zeros((ROWS, LANES), F32)
        self.speed = {}
        self.velocity = {}
        self.pressure = zero

    def flux(self, var, direction, value, cotangent):
        gas = self.gas
        term = cotangent * value
        if var == ENERGY:
            term = term + cotangent * gas.pressure
            self.pressure = self.pressure + cotangent * gas.velocity[direction]
        if var == SPECIES + direction:
            self.pressure = self.pressure + cotangent
        held = self.velocity.get(direction)
        self.velocity[direction] = term if held is None else held + term
        return cotangent * gas.velocity[direction]

    def wave(self, direction, term):
        held = self.speed.get(direction)
        self.speed[direction] = term if held is None else held + term

    def close(self):
        gas = self.gas
        inverse, pressure = gas.inverse, self.pressure
        into = jnp.zeros((ROWS, LANES), F32)
        for direction, term in self.speed.items():
            scaled = term / gas.speed[direction]
            self.velocity[direction] = self.velocity[direction] + scaled * gas.velocity[direction]
            pressure = pressure + 0.7 * scaled * inverse
            into = into + 0.7 * scaled * gas.pressure
        for direction, term in self.velocity.items():
            into = into + term * gas.momenta[direction]
        into = into - 0.2 * pressure * gas.square
        self.species = -inverse * inverse * into
        self.momentum = []
        for e in range(3):
            term = -0.4 * pressure * gas.momenta[e]
            if e in self.velocity:
                term = term + self.velocity[e]
            self.momentum.append(term * inverse)
        self.energy = 0.4 * pressure

    def rest(self, var):
        if var < SPECIES:
            return self.species
        return self.energy if var == ENERGY else self.momentum[var - SPECIES]


def spread(lines):
    place = lax.broadcasted_iota(jnp.int32, (8, 16), 0)
    element = lax.broadcasted_iota(jnp.int32, (8, 16), 1)
    left = lane_of(8) < 64
    columns = []
    for column in range(2):
        line = jnp.broadcast_to(lines[column], (8, 16))
        picked = [
            jnp.sum(jnp.where(element == 2 * place + half, line, 0.0), axis=1, keepdims=True)
            for half in range(2)
        ]
        columns.append(jnp.where(left, picked[0], picked[1]))
    return jnp.concatenate(columns, axis=0)


def spread_rate(coupling, source, target):
    return jnp.broadcast_to(coupling[source, target : target + 1, :], (ROWS, LANES))


def damping(flags, scales, section):
    lines = []
    for column in range(2):
        at = (section, column)
        lines.append(jnp.where(flags[at] == 1, scales[at], 1.0))
    return spread(lines)


def limited(field, factor, high, low, table, transposed):
    for var in range(VARS):
        value = field(var)
        if transposed:
            value = (1.0 - factor) * value
        high[block(var), :], low[block(var), :] = split(value)
    means = product(high[...], low[...], table)

    def get(var):
        mean = means[ROWS * var : ROWS * (var + 1)]
        if transposed:
            return factor * field(var) + mean
        return mean + factor * (field(var) - mean)

    return get


def start_kernel(count, *refs):
    there, here, sent, arrived = refs[:count], refs[count : 2 * count], refs[2 * count : -1], refs[-1]
    copies = [pltpu.make_async_copy(there[k], here[k], arrived.at[k]) for k in range(count)]
    for copy in copies:
        copy.start()
    copies[0].wait()
    pack(lambda v: here[0][v], sent)
    for copy in copies[1:]:
        copy.wait()


def setup_kernel(columns, lines, adjoint, rates, codes, flags, scales, mean_t, lam, yb, xb, ya, xa, walls, factors, coupling, high, low):
    row = lax.broadcasted_iota(jnp.int32, (SPECIES, SPECIES), 0)
    same = row == lax.broadcasted_iota(jnp.int32, (SPECIES, SPECIES), 1)
    off_diag = jnp.where(same, 0.0, rates[...])
    leaving = jnp.sum(off_diag, axis=0, keepdims=True)
    full = jnp.where(same, -jnp.broadcast_to(leaving, (SPECIES, SPECIES)), off_diag)
    for source in range(SPECIES):
        coupling[source] = jnp.broadcast_to(full[:, source : source + 1], (SPECIES, LANES))
    for section in range(3):
        factors[section] = damping(flags, scales, section)
    get = limited(lambda v: adjoint[v], factors[2], high, low, mean_t, True)
    for var in range(VARS):
        lam[var] = (2.0 / 3.0) * get(var)
    pack(lambda v: lam[v], (yb, xb, ya, xa))
    code = spread([codes[column].astype(F32) for column in range(2)]).astype(jnp.int32)
    row = lax.broadcasted_iota(jnp.int32, (ROWS, LANES), 0)
    lane = lane_of()
    at_x = jnp.zeros((ROWS, LANES), jnp.int32) + lax.axis_index("gx")
    at_y = jnp.zeros((ROWS, LANES), jnp.int32) + lax.axis_index("gy")
    both = jnp.logical_and
    ends = (
        (both(at_x == 0, row < 8), both(at_x == columns - 1, row >= 8)),
        (at_y == 0, at_y == lines - 1),
        (both(row % 8 == 0, lane < 64), both(row % 8 == 7, lane >= 64)),
    )
    for d in range(3):
        index = node_index(d)
        low = (1 - 2 * ((code >> (2 * d)) & 1)).astype(F32)
        high = (1 - 2 * ((code >> (2 * d + 1)) & 1)).astype(F32)
        wall = jnp.where(both(ends[d][0], index == 0), low, 0.0)
        walls[d] = jnp.where(both(ends[d][1], index == 3), high, wall)


def volume_kernel(mix, coupling, state, start, walls, table, out, near, high, low, total):
    from_start, from_here = mix
    gas = Gas(lambda v: state[v], (0, 1, 2))
    for var in range(VARS):
        value = state[var]
        for d in range(3):
            flux = value * gas.velocity[d]
            if var == SPECIES + d:
                flux = flux + gas.pressure
            if var == ENERGY:
                flux = flux + gas.pressure * gas.velocity[d]
            at = pl.ds(LANES * d, LANES)
            high[block(var), at], low[block(var), at] = split(flux)
    total[...] = product(high[...], low[...], table)
    face = Face(walls[2], 2)
    for var in range(VARS):
        value = state[var]
        near[var] = face.outside(var, value, *shift_z(value))
    gain = face_gain(face, 2, gas, Gas(lambda v: near[v], (2,)))
    for var in range(VARS):
        value = state[var]
        change = gain(var, value, near[var]) - total[block(var), :]
        if var < SPECIES:
            for other in range(SPECIES):
                change = change + spread_rate(coupling, other, var) * state[other]
        here = from_here * value + (from_here * STEP) * change
        if from_start:
            here = here + from_start * start[var]
        out[var] = here


def fetch_near(state, walls, received, near_x, near_y):
    face_x, face_y = Face(walls[0], 0), Face(walls[1], 1)
    for var in range(VARS):
        value = state[var]
        near_x[var] = face_x.outside(var, value, *received.along_x(var, value))
        near_y[var] = face_y.outside(var, value, *received.along_y(var))


def face_kernel(section, share, last, state, inner, walls, factors, mean, *refs):
    along = ()
    if last:
        near_x, near_y, out, high, low = refs
    else:
        along = refs[4:-9]
        xa, xb, ya, yb = refs[:4]
        out, near_x, near_y, sa, sb, sc, sd, high, low = refs[-9:]
        fetch_near(state, walls, Received((xa, xb, ya, yb)), near_x, near_y)
    gas = Gas(lambda v: state[v], (0, 1))
    gain_x = face_gain(Face(walls[0], 0), 0, gas, Gas(lambda v: near_x[v], (0,)))
    gain_y = face_gain(Face(walls[1], 1), 1, gas, Gas(lambda v: near_y[v], (1,)))
    for var in range(VARS):
        value = state[var]
        change = gain_x(var, value, near_x[var]) + gain_y(var, value, near_y[var])
        out[var] = inner[var] + (share * STEP) * change
    get = limited(lambda v: out[v], factors[section], high, low, mean, False)
    for var in range(VARS):
        out[var] = get(var)
    if not last:
        pack(lambda v: out[v], (sa, sb, sc, sd))
        for held, sent in zip(along, (sa, sb, sc, sd)):
            sent[GROUPS:] = held[...]


def back_volume_kernel(coupling, state, lam, near, walls, table, out, high, low, total):
    for var in range(VARS):
        high[block(var), :], low[block(var), :] = split(lam[var])
    total[...] = product(high[...], low[...], table)
    gas = Gas(lambda v: state[v], (0, 1, 2))
    other = Gas(lambda v: near[v], (2,))
    face = Face(walls[2], 2)
    speeds = gas.speed[2] + other.speed[2]
    back = Back(gas)
    for var in range(VARS):
        value, own = state[var], lam[var]
        outside = face.outside(var, own, *shift_z(own))
        part = back.flux(var, 0, value, -total[block(var), pl.ds(0, LANES)])
        part = part + back.flux(var, 1, value, -total[block(var), pl.ds(LANES, LANES)])
        part = part + back.flux(
            var, 2, value, -total[block(var), pl.ds(2 * LANES, LANES)] - face.three * (own + outside)
        )
        jump = face.half * (outside - own)
        back.wave(2, jump * (value - near[var]))
        out[var] = part + speeds * jump
    back.close()
    for var in range(VARS):
        change = out[var] + back.rest(var)
        if var < SPECIES:
            for other_var in range(SPECIES):
                change = change + spread_rate(coupling, var, other_var) * lam[other_var]
        out[var] = lam[var] + STEP * change


def back_faces(state, lam, near_x, near_y, walls, received, inner, out):
    gas = Gas(lambda v: state[v], (0, 1))
    faces = (Face(walls[0], 0), Face(walls[1], 1))
    nears = (near_x, near_y)
    speeds = [gas.speed[d] + Gas(lambda v, d=d: nears[d][v], (d,)).speed[d] for d in range(2)]
    back = Back(gas)
    for var in range(VARS):
        value, own = state[var], lam[var]
        part = inner[var]
        for d in range(2):
            sides = received.along_x(var, own) if d == 0 else received.along_y(var)
            outside = faces[d].outside(var, own, *sides)
            part = part + STEP * back.flux(var, d, value, -faces[d].three * (own + outside))
            jump = faces[d].half * (outside - own)
            back.wave(d, jump * (value - nears[d][var]))
            part = part + STEP * (speeds[d] * jump)
        out[var] = part
    back.close()
    for var in range(VARS):
        out[var] = out[var] + STEP * back.rest(var)


def turn_kernel(state, lam, inner, walls, factors, mean_t, *refs):
    got = refs[:4]
    below, carry, near_x, near_y, sa, sb, sc, sd, high, low, work = refs[4:]
    fetch_near(state, walls, Received(got), near_x, near_y)
    back_faces(state, lam, near_x, near_y, walls, Received(got, 1), inner, work)
    get = limited(lambda v: work[v], factors[1], high, low, mean_t, True)
    for var in range(VARS):
        reverse = get(var)
        carry[var] = 0.5 * lam[var] + 0.75 * reverse
        below[var] = 0.25 * reverse
    pack(lambda v: below[v], (sa, sb, sc, sd))


def middle_kernel(state, lam, inner, near_x, near_y, walls, factors, mean_t, *refs):
    la, lb, lc, ld, below, sa, sb, sc, sd, high, low, work = refs
    back_faces(state, lam, near_x, near_y, walls, Received((la, lb, lc, ld)), inner, work)
    get = limited(lambda v: work[v], factors[0], high, low, mean_t, True)
    for var in range(VARS):
        below[var] = get(var)
    pack(lambda v: below[v], (sa, sb, sc, sd))


def end_kernel(state, lam, inner, near_x, near_y, carry, walls, la, lb, lc, ld, out):
    back_faces(state, lam, near_x, near_y, walls, Received((la, lb, lc, ld)), inner, out)
    for var in range(VARS):
        out[var] = out[var] + carry[var]


FIELD = (VARS, ROWS, LANES)
TABLE = (3, ROWS, LANES)


def call(kernel, inputs, outputs, scratch=()):
    return pl.pallas_call(
        kernel,
        in_specs=[pl.BlockSpec(memory_space=pltpu.VMEM)] * len(inputs),
        out_specs=[pl.BlockSpec(memory_space=pltpu.VMEM)] * len(outputs),
        out_shape=[jax.ShapeDtypeStruct(shape, F32) for shape in outputs],
        scratch_shapes=list(scratch),
        compiler_params=pltpu.CompilerParams(vmem_limit_bytes=8 << 20),
        name=getattr(kernel, "func", kernel).__name__,
    )(*inputs)


def packs(parts):
    return [(parts * GROUPS, ROWS, LANES), (parts * GROUPS, 8, LANES), (parts * GROUPS, ROWS, LANES), (parts * GROUPS, 8, LANES)]


def halved(width):
    return [pltpu.VMEM((VARS * ROWS, width), BF16)] * 2


def exchange(sent):
    columns, lines = lax.axis_size("gx"), lax.axis_size("gy")

    def swap(values, along_x, first):
        moves = []
        for x in range(columns):
            for y in range(lines):
                at, count, other = (x, columns, y) if along_x else (y, lines, x)
                if at % 2 == first:
                    mate, across = at + 1, other
                else:
                    mate, across = at - 1, other
                if mate < 0 or mate >= count:
                    mate, across = at, other ^ 1
                to = (mate, across) if along_x else (across, mate)
                moves.append((x * lines + y, to[0] * lines + to[1]))
        return lax.ppermute(values, ("gx", "gy"), moves)

    yb, xb, ya, xa = sent
    yb = swap(yb, False, 1)
    xb = swap(xb, True, 1)
    ya = swap(ya, False, 0)
    xa = swap(xa, True, 0)
    return [yb, xb, ya, xa]


def per_device(state_start, adjoint_end, limiter_flags, limiter_scales, face_codes, reaction_rates):
    forward, backward, mean, mean_t = [halves(table) for table in node_tables()]
    q0 = state_start.reshape(FIELD)
    adjoint = adjoint_end.reshape(FIELD)
    narrow, wide = halved(LANES), halved(3 * LANES)
    total = [pltpu.VMEM((VARS * ROWS, LANES), F32)]
    total3 = [pltpu.VMEM((VARS * ROWS, 3 * LANES), F32)]
    work = [pltpu.VMEM(FIELD, F32)]

    held = [q0, adjoint, reaction_rates, face_codes, limiter_flags, limiter_scales]
    held += [mean_t, forward, mean, backward]
    got = pl.pallas_call(
        functools.partial(start_kernel, len(held)),
        in_specs=[pl.BlockSpec(memory_space=pltpu.HBM)] * len(held),
        out_specs=[pl.BlockSpec(memory_space=pltpu.VMEM)] * (len(held) + 4),
        out_shape=[jax.ShapeDtypeStruct(v.shape, v.dtype) for v in held]
        + [jax.ShapeDtypeStruct(shape, F32) for shape in packs(1)],
        scratch_shapes=[pltpu.SemaphoreType.DMA((len(held),))],
        compiler_params=pltpu.CompilerParams(vmem_limit_bytes=8 << 20),
        name="start_kernel",
    )(*[pltpu.with_memory_space_constraint(v, pltpu.HBM) for v in held])
    q0, adjoint, rates, codes, flags, scales, mean_t, forward, mean, backward = got[: len(held)]
    got = exchange(got[len(held) :])
    size = functools.partial(setup_kernel, lax.axis_size("gx"), lax.axis_size("gy"))
    lam3, *along, walls, factors, coupling = call(
        size,
        [adjoint, rates, codes, flags, scales, mean_t],
        [FIELD] + packs(1) + [TABLE, TABLE, (SPECIES, SPECIES, LANES)],
        narrow,
    )

    def inner(mix, state):
        kernel = functools.partial(volume_kernel, mix)
        return call(kernel, [coupling, state, q0, walls, forward], [FIELD, FIELD], wide + total)

    def back_inner(state, lam, near):
        return call(
            back_volume_kernel, [coupling, state, lam, near, walls, backward], [FIELD], narrow + total3
        )[0]

    def outer(section, share, state, part, got, along=()):
        kernel = functools.partial(face_kernel, section, share, False)
        out, near_x, near_y, *sent = call(
            kernel, [state, part, walls, factors, mean, *got, *along],
            [FIELD] * 3 + packs(2 if along else 1),
            narrow,
        )
        return out, near_x, near_y, sent

    part, z0 = inner((0.0, 1.0), q0)
    q1, x0, y0, sent = outer(0, 1.0, q0, part, got)
    got = exchange(sent)
    part, z1 = inner((0.75, 0.25), q1)
    q2, x1, y1, sent = outer(1, 0.25, q1, part, got, along)
    got = exchange(sent)
    part, z2 = inner((1.0 / 3.0, 2.0 / 3.0), q2)
    back = back_inner(q2, lam3, z2)
    lam2, carry, x2, y2, *sent = call(
        turn_kernel,
        [q2, lam3, back, walls, factors, mean_t, *got],
        [FIELD] * 4 + packs(1),
        narrow + work,
    )
    got = exchange(sent)
    last = functools.partial(face_kernel, 2, 2.0 / 3.0, True)
    state_end = call(last, [q2, part, walls, factors, mean, x2, y2], [FIELD], narrow)[0]
    back = back_inner(q1, lam2, z1)
    lam1, *sent = call(
        middle_kernel,
        [q1, lam2, back, x1, y1, walls, factors, mean_t, *got],
        [FIELD] + packs(1),
        narrow + work,
    )
    got = exchange(sent)
    back = back_inner(q0, lam1, z0)
    adjoint_start = call(end_kernel, [q0, lam1, back, x0, y0, carry, walls, *got], [FIELD])[0]
    return state_end.reshape(state_start.shape), adjoint_start.reshape(state_start.shape)


def solution(mesh):
    field = P(None, "gx", "gy", None)
    return jax.shard_map(
        per_device,
        mesh=mesh,
        in_specs=(field, field, field, field, P("gx", "gy", None), P()),
        out_specs=(field, field),
        check_vma=False,
    )
```

```python
import functools

import jax
import jax.numpy as jnp
import numpy as np
from jax import lax
from jax.experimental import pallas as pl
from jax.experimental.pallas import tpu as pltpu
from jax.sharding import PartitionSpec as P

SPECIES = 21
VARS = 25
ENERGY = 24
GROUPS = 7
STEP = 0.008
F32 = jnp.float32
BF16 = jnp.bfloat16
ROWS = 16
LANES = 128


def node_tables():
    points = np.array([-1.0, -1.0 / np.sqrt(5.0), 1.0 / np.sqrt(5.0), 1.0])
    bary = np.array([1.0 / np.prod([points[a] - points[b] for b in range(4) if b != a]) for a in range(4)])
    deriv = np.zeros((4, 4))
    for a in range(4):
        for b in range(4):
            if a != b:
                deriv[a, b] = bary[b] / bary[a] / (points[a] - points[b])
        deriv[a, a] = -np.sum(deriv[a])
    eye = np.eye(4)
    pair = np.eye(2)
    ops = [
        np.kron(np.kron(deriv.T, eye), eye),
        np.kron(np.kron(eye, deriv.T), eye),
        np.kron(np.kron(eye, eye), deriv.T),
    ]
    grads = [np.kron(pair, op) for op in ops]
    whole = np.array([1.0, 5.0, 5.0, 1.0])
    cube = np.kron(np.kron(whole, whole), whole) / 2048.0
    mean = np.kron(pair, np.repeat(cube[:, None], 64, axis=1))
    forward = np.concatenate(grads, axis=0)
    backward = np.concatenate([g.T for g in grads], axis=1)
    return forward, backward, mean, mean.T


def stacked(table):
    return jnp.asarray(np.concatenate([table, table], axis=0).astype(jnp.bfloat16))


def halves(table):
    table = np.asarray(table, np.float32)
    high = table.astype(jnp.bfloat16)
    low = (table - high.astype(np.float32)).astype(jnp.bfloat16)
    return jnp.asarray(np.stack([high, low]))


def split(values):
    high = values.astype(BF16)
    return high, (values - high.astype(F32)).astype(BF16)


def product(high, low, table):
    dot = functools.partial(jnp.dot, preferred_element_type=F32)
    return dot(high, table[0]) + dot(high, table[1]) + dot(low, table[0])


def roll(values, shift, axis):
    shift = shift % values.shape[axis]
    return values if shift == 0 else pltpu.roll(values, shift, axis)


def lane_of(rows=ROWS):
    return lax.broadcasted_iota(jnp.int32, (rows, LANES), 1)


def node_index(direction, rows=ROWS):
    return (lane_of(rows) >> (4, 2, 0)[direction]) & 3


def block(var):
    return pl.ds(ROWS * var, ROWS)


class Face:
    def __init__(self, wall, direction):
        index = node_index(direction)
        inside = wall == 0.0
        self.low = jnp.logical_and(index == 0, inside)
        self.high = jnp.logical_and(index == 3, inside)
        self.sign = jnp.where(wall < 0.0, -1.0, 1.0)
        live = jnp.where(wall > 0.0, 0.0, 1.0)
        self.three = jnp.where(index == 0, 3.0, jnp.where(index == 3, -3.0, 0.0)) * live
        self.half = jnp.where(jnp.logical_or(index == 0, index == 3), 1.5, 0.0) * live
        self.momentum = SPECIES + direction

    def outside(self, var, own, low, high):
        edge = own * self.sign if var == self.momentum else own
        return jnp.where(self.low, low, jnp.where(self.high, high, edge))


def shift_z(values):
    first = lane_of() < 64
    low = roll(values, 61, 1)
    low = jnp.where(first, roll(low, 1, 0), low)
    high = roll(values, 67, 1)
    high = jnp.where(first, high, roll(high, ROWS - 1, 0))
    return low, high


class Received:
    def __init__(self, refs, part=0):
        even_x = (jnp.zeros((8, LANES), jnp.int32) + lax.axis_index("gx") % 2) == 0
        even_y = (jnp.zeros((ROWS, LANES), jnp.int32) + lax.axis_index("gy") % 2) == 0
        yb, xb, ya, xa = refs
        self.packs = []
        for group in range(GROUPS):
            at = part * GROUPS + group
            a, b, c, d = xa[at], xb[at], ya[at], yb[at]
            self.packs.append(
                (
                    jnp.where(even_x, b, a),
                    jnp.where(even_x, a, b),
                    jnp.where(even_y, d, c),
                    jnp.where(even_y, c, d),
                )
            )

    def along_x(self, var, own):
        group, slot = divmod(var, 4)
        low, high = self.packs[group][:2]
        first, second = own[:8], own[8:]
        return (
            jnp.concatenate([roll(low, -16 * slot, 1), roll(first, -48, 1)], axis=0),
            jnp.concatenate([roll(second, 48, 1), roll(high, 16 * (3 - slot), 1)], axis=0),
        )

    def along_y(self, var):
        group, slot = divmod(var, 4)
        low, high = self.packs[group][2:]
        return roll(low, -4 * slot, 1), roll(high, 4 * (3 - slot), 1)


def pack(field, refs, part=0):
    even_x = (jnp.zeros((8, LANES), jnp.int32) + lax.axis_index("gx") % 2) == 0
    even_y = (jnp.zeros((ROWS, LANES), jnp.int32) + lax.axis_index("gy") % 2) == 0
    yb, xb, ya, xa = refs
    spot_x, spot_y = node_index(0, 8), node_index(1)

    def merged(spot, pieces):
        out = pieces[3]
        for slot in (2, 1, 0):
            out = jnp.where(spot == slot, pieces[slot], out)
        return out

    for group in range(GROUPS):
        at = part * GROUPS + group
        own = [field(min(4 * group + slot, ENERGY)) for slot in range(4)]
        if group == GROUPS - 1:
            x_low, x_high = own[0][:8], roll(own[0][8:], -48, 1)
            y_low, y_high = own[0], roll(own[0], -12, 1)
        else:
            x_low = merged(spot_x, [roll(own[s][:8], 16 * s, 1) for s in range(4)])
            x_high = merged(spot_x, [roll(own[s][8:], 16 * (s - 3), 1) for s in range(4)])
            y_low = merged(spot_y, [roll(own[s], 4 * s, 1) for s in range(4)])
            y_high = merged(spot_y, [roll(own[s], 4 * (s - 3), 1) for s in range(4)])
        xa[at] = jnp.where(even_x, x_high, x_low)
        xb[at] = jnp.where(even_x, x_low, x_high)
        ya[at] = jnp.where(even_y, y_high, y_low)
        yb[at] = jnp.where(even_y, y_low, y_high)


class Gas:
    def __init__(self, field, directions):
        density = field(0)
        for var in range(1, SPECIES):
            density = density + field(var)
        self.inverse = 1.0 / density
        self.momenta = [field(SPECIES + e) for e in range(3)]
        m0, m1, m2 = self.momenta
        self.square = m0 * m0 + m1 * m1 + m2 * m2
        self.pressure = 0.4 * (field(ENERGY) - 0.5 * self.square * self.inverse)
        self.velocity = {d: self.momenta[d] * self.inverse for d in directions}
        sound = 1.4 * self.pressure * self.inverse
        self.speed = {d: jnp.sqrt(self.velocity[d] * self.velocity[d] + sound) for d in directions}


def face_gain(face, direction, own, other):
    weight = face.half * (own.speed[direction] + other.speed[direction])
    u_in, u_out = own.velocity[direction], other.velocity[direction]
    take, leave = face.three * u_out + weight, face.three * u_in + weight

    def gain(var, inside, outside):
        total = outside * take - inside * leave
        if var == face.momentum:
            total = total + face.three * (other.pressure - own.pressure)
        if var == ENERGY:
            total = total + face.three * (other.pressure * u_out - own.pressure * u_in)
        return total

    return gain


class Back:
    def __init__(self, gas):
        self.gas = gas
        zero = jnp.zeros((ROWS, LANES), F32)
        self.speed = {}
        self.velocity = {}
        self.pressure = zero

    def flux(self, var, direction, value, cotangent):
        gas = self.gas
        term = cotangent * value
        if var == ENERGY:
            term = term + cotangent * gas.pressure
            self.pressure = self.pressure + cotangent * gas.velocity[direction]
        if var == SPECIES + direction:
            self.pressure = self.pressure + cotangent
        held = self.velocity.get(direction)
        self.velocity[direction] = term if held is None else held + term
        return cotangent * gas.velocity[direction]

    def wave(self, direction, term):
        held = self.speed.get(direction)
        self.speed[direction] = term if held is None else held + term

    def close(self):
        gas = self.gas
        inverse, pressure = gas.inverse, self.pressure
        into = jnp.zeros((ROWS, LANES), F32)
        for direction, term in self.speed.items():
            scaled = term / gas.speed[direction]
            self.velocity[direction] = self.velocity[direction] + scaled * gas.velocity[direction]
            pressure = pressure + 0.7 * scaled * inverse
            into = into + 0.7 * scaled * gas.pressure
        for direction, term in self.velocity.items():
            into = into + term * gas.momenta[direction]
        into = into - 0.2 * pressure * gas.square
        self.species = -inverse * inverse * into
        self.momentum = []
        for e in range(3):
            term = -0.4 * pressure * gas.momenta[e]
            if e in self.velocity:
                term = term + self.velocity[e]
            self.momentum.append(term * inverse)
        self.energy = 0.4 * pressure

    def rest(self, var):
        if var < SPECIES:
            return self.species
        return self.energy if var == ENERGY else self.momentum[var - SPECIES]


def spread(lines):
    place = lax.broadcasted_iota(jnp.int32, (8, 16), 0)
    element = lax.broadcasted_iota(jnp.int32, (8, 16), 1)
    left = lane_of(8) < 64
    columns = []
    for column in range(2):
        line = jnp.broadcast_to(lines[column], (8, 16))
        picked = [
            jnp.sum(jnp.where(element == 2 * place + half, line, 0.0), axis=1, keepdims=True)
            for half in range(2)
        ]
        columns.append(jnp.where(left, picked[0], picked[1]))
    return jnp.concatenate(columns, axis=0)


def spread_rate(coupling, source, target):
    return jnp.broadcast_to(coupling[source, target : target + 1, :], (ROWS, LANES))


def damping(flags, scales, section):
    lines = []
    for column in range(2):
        at = (section, column)
        lines.append(jnp.where(flags[at] == 1, scales[at], 1.0))
    return spread(lines)


def limited(field, factor, both, table, transposed):
    for var in range(VARS):
        value = field(var)
        if transposed:
            value = (1.0 - factor) * value
        both[block(var), pl.ds(0, LANES)], both[block(var), pl.ds(LANES, LANES)] = split(value)
    means = jnp.dot(both[...], table[...], preferred_element_type=F32) * (2048.0 / 1728.0)

    def get(var):
        mean = means[ROWS * var : ROWS * (var + 1)]
        if transposed:
            return factor * field(var) + mean
        return mean + factor * (field(var) - mean)

    return get


def start_kernel(count, *refs):
    there, here, sent, arrived = refs[:count], refs[count : 2 * count], refs[2 * count : -1], refs[-1]
    copies = [pltpu.make_async_copy(there[k], here[k], arrived.at[k]) for k in range(count)]
    for copy in copies:
        copy.start()
    copies[0].wait()
    pack(lambda v: here[0][v], sent)
    for copy in copies[1:]:
        copy.wait()


def setup_kernel(columns, lines, adjoint, rates, codes, flags, scales, mean_t, lam, yb, xb, ya, xa, walls, factors, coupling, both):
    row = lax.broadcasted_iota(jnp.int32, (SPECIES, SPECIES), 0)
    same = row == lax.broadcasted_iota(jnp.int32, (SPECIES, SPECIES), 1)
    off_diag = jnp.where(same, 0.0, rates[...])
    leaving = jnp.sum(off_diag, axis=0, keepdims=True)
    full = jnp.where(same, -jnp.broadcast_to(leaving, (SPECIES, SPECIES)), off_diag)
    for source in range(SPECIES):
        coupling[source] = jnp.broadcast_to(full[:, source : source + 1], (SPECIES, LANES))
    for section in range(3):
        factors[section] = damping(flags, scales, section)
    get = limited(lambda v: adjoint[v], factors[2], both, mean_t, True)
    for var in range(VARS):
        lam[var] = (2.0 / 3.0) * get(var)
    pack(lambda v: lam[v], (yb, xb, ya, xa))
    code = spread([codes[column].astype(F32) for column in range(2)]).astype(jnp.int32)
    row = lax.broadcasted_iota(jnp.int32, (ROWS, LANES), 0)
    lane = lane_of()
    at_x = jnp.zeros((ROWS, LANES), jnp.int32) + lax.axis_index("gx")
    at_y = jnp.zeros((ROWS, LANES), jnp.int32) + lax.axis_index("gy")
    both = jnp.logical_and
    ends = (
        (both(at_x == 0, row < 8), both(at_x == columns - 1, row >= 8)),
        (at_y == 0, at_y == lines - 1),
        (both(row % 8 == 0, lane < 64), both(row % 8 == 7, lane >= 64)),
    )
    for d in range(3):
        index = node_index(d)
        low = (1 - 2 * ((code >> (2 * d)) & 1)).astype(F32)
        high = (1 - 2 * ((code >> (2 * d + 1)) & 1)).astype(F32)
        wall = jnp.where(both(ends[d][0], index == 0), low, 0.0)
        walls[d] = jnp.where(both(ends[d][1], index == 3), high, wall)


def volume_kernel(mix, coupling, state, start, walls, table, out, near, high, low, total):
    from_start, from_here = mix
    gas = Gas(lambda v: state[v], (0, 1, 2))
    for var in range(VARS):
        value = state[var]
        for d in range(3):
            flux = value * gas.velocity[d]
            if var == SPECIES + d:
                flux = flux + gas.pressure
            if var == ENERGY:
                flux = flux + gas.pressure * gas.velocity[d]
            at = pl.ds(LANES * d, LANES)
            high[block(var), at], low[block(var), at] = split(flux)
    total[...] = product(high[...], low[...], table)
    face = Face(walls[2], 2)
    for var in range(VARS):
        value = state[var]
        near[var] = face.outside(var, value, *shift_z(value))
    gain = face_gain(face, 2, gas, Gas(lambda v: near[v], (2,)))
    for var in range(VARS):
        value = state[var]
        change = gain(var, value, near[var]) - total[block(var), :]
        if var < SPECIES:
            for other in range(SPECIES):
                change = change + spread_rate(coupling, other, var) * state[other]
        here = from_here * value + (from_here * STEP) * change
        if from_start:
            here = here + from_start * start[var]
        out[var] = here


def fetch_near(state, walls, received, near_x, near_y):
    face_x, face_y = Face(walls[0], 0), Face(walls[1], 1)
    for var in range(VARS):
        value = state[var]
        near_x[var] = face_x.outside(var, value, *received.along_x(var, value))
        near_y[var] = face_y.outside(var, value, *received.along_y(var))


def face_kernel(section, share, last, state, inner, walls, factors, mean, *refs):
    along = ()
    if last:
        near_x, near_y, out, both = refs
    else:
        along = refs[4:-8]
        xa, xb, ya, yb = refs[:4]
        out, near_x, near_y, sa, sb, sc, sd, both = refs[-8:]
        fetch_near(state, walls, Received((xa, xb, ya, yb)), near_x, near_y)
    gas = Gas(lambda v: state[v], (0, 1))
    gain_x = face_gain(Face(walls[0], 0), 0, gas, Gas(lambda v: near_x[v], (0,)))
    gain_y = face_gain(Face(walls[1], 1), 1, gas, Gas(lambda v: near_y[v], (1,)))
    for var in range(VARS):
        value = state[var]
        change = gain_x(var, value, near_x[var]) + gain_y(var, value, near_y[var])
        out[var] = inner[var] + (share * STEP) * change
    get = limited(lambda v: out[v], factors[section], both, mean, False)
    for var in range(VARS):
        out[var] = get(var)
    if not last:
        pack(lambda v: out[v], (sa, sb, sc, sd))
        for held, sent in zip(along, (sa, sb, sc, sd)):
            sent[GROUPS:] = held[...]


def back_volume_kernel(coupling, state, lam, near, walls, table, out, high, low, total):
    for var in range(VARS):
        high[block(var), :], low[block(var), :] = split(lam[var])
    total[...] = product(high[...], low[...], table)
    gas = Gas(lambda v: state[v], (0, 1, 2))
    other = Gas(lambda v: near[v], (2,))
    face = Face(walls[2], 2)
    speeds = gas.speed[2] + other.speed[2]
    back = Back(gas)
    for var in range(VARS):
        value, own = state[var], lam[var]
        outside = face.outside(var, own, *shift_z(own))
        part = back.flux(var, 0, value, -total[block(var), pl.ds(0, LANES)])
        part = part + back.flux(var, 1, value, -total[block(var), pl.ds(LANES, LANES)])
        part = part + back.flux(
            var, 2, value, -total[block(var), pl.ds(2 * LANES, LANES)] - face.three * (own + outside)
        )
        jump = face.half * (outside - own)
        back.wave(2, jump * (value - near[var]))
        out[var] = part + speeds * jump
    back.close()
    for var in range(VARS):
        change = out[var] + back.rest(var)
        if var < SPECIES:
            for other_var in range(SPECIES):
                change = change + spread_rate(coupling, var, other_var) * lam[other_var]
        out[var] = lam[var] + STEP * change


def back_faces(state, lam, near_x, near_y, walls, received, inner, out):
    gas = Gas(lambda v: state[v], (0, 1))
    faces = (Face(walls[0], 0), Face(walls[1], 1))
    nears = (near_x, near_y)
    speeds = [gas.speed[d] + Gas(lambda v, d=d: nears[d][v], (d,)).speed[d] for d in range(2)]
    back = Back(gas)
    for var in range(VARS):
        value, own = state[var], lam[var]
        part = inner[var]
        for d in range(2):
            sides = received.along_x(var, own) if d == 0 else received.along_y(var)
            outside = faces[d].outside(var, own, *sides)
            part = part + STEP * back.flux(var, d, value, -faces[d].three * (own + outside))
            jump = faces[d].half * (outside - own)
            back.wave(d, jump * (value - nears[d][var]))
            part = part + STEP * (speeds[d] * jump)
        out[var] = part
    back.close()
    for var in range(VARS):
        out[var] = out[var] + STEP * back.rest(var)


def turn_kernel(state, lam, inner, walls, factors, mean_t, *refs):
    got = refs[:4]
    below, carry, near_x, near_y, sa, sb, sc, sd, both, work = refs[4:]
    fetch_near(state, walls, Received(got), near_x, near_y)
    back_faces(state, lam, near_x, near_y, walls, Received(got, 1), inner, work)
    get = limited(lambda v: work[v], factors[1], both, mean_t, True)
    for var in range(VARS):
        reverse = get(var)
        carry[var] = 0.5 * lam[var] + 0.75 * reverse
        below[var] = 0.25 * reverse
    pack(lambda v: below[v], (sa, sb, sc, sd))


def middle_kernel(state, lam, inner, near_x, near_y, walls, factors, mean_t, *refs):
    la, lb, lc, ld, below, sa, sb, sc, sd, both, work = refs
    back_faces(state, lam, near_x, near_y, walls, Received((la, lb, lc, ld)), inner, work)
    get = limited(lambda v: work[v], factors[0], both, mean_t, True)
    for var in range(VARS):
        below[var] = get(var)
    pack(lambda v: below[v], (sa, sb, sc, sd))


def end_kernel(state, lam, inner, near_x, near_y, carry, walls, la, lb, lc, ld, out):
    back_faces(state, lam, near_x, near_y, walls, Received((la, lb, lc, ld)), inner, out)
    for var in range(VARS):
        out[var] = out[var] + carry[var]


FIELD = (VARS, ROWS, LANES)
TABLE = (3, ROWS, LANES)


def call(kernel, inputs, outputs, scratch=()):
    return pl.pallas_call(
        kernel,
        in_specs=[pl.BlockSpec(memory_space=pltpu.VMEM)] * len(inputs),
        out_specs=[pl.BlockSpec(memory_space=pltpu.VMEM)] * len(outputs),
        out_shape=[jax.ShapeDtypeStruct(shape, F32) for shape in outputs],
        scratch_shapes=list(scratch),
        compiler_params=pltpu.CompilerParams(vmem_limit_bytes=8 << 20),
        name=getattr(kernel, "func", kernel).__name__,
    )(*inputs)


def packs(parts):
    return [(parts * GROUPS, ROWS, LANES), (parts * GROUPS, 8, LANES), (parts * GROUPS, ROWS, LANES), (parts * GROUPS, 8, LANES)]


def halved(width):
    return [pltpu.VMEM((VARS * ROWS, width), BF16)] * 2


def exchange(sent):
    columns, lines = lax.axis_size("gx"), lax.axis_size("gy")

    def swap(values, along_x, first):
        moves = []
        for x in range(columns):
            for y in range(lines):
                at, count, other = (x, columns, y) if along_x else (y, lines, x)
                if at % 2 == first:
                    mate, across = at + 1, other
                else:
                    mate, across = at - 1, other
                if mate < 0 or mate >= count:
                    mate, across = at, other ^ 1
                to = (mate, across) if along_x else (across, mate)
                moves.append((x * lines + y, to[0] * lines + to[1]))
        return lax.ppermute(values, ("gx", "gy"), moves)

    yb, xb, ya, xa = sent
    yb = swap(yb, False, 1)
    xb = swap(xb, True, 1)
    ya = swap(ya, False, 0)
    xa = swap(xa, True, 0)
    return [yb, xb, ya, xa]


def per_device(state_start, adjoint_end, limiter_flags, limiter_scales, face_codes, reaction_rates):
    forward, backward, mean, mean_t = node_tables()
    forward, backward, mean, mean_t = halves(forward), halves(backward), stacked(mean), stacked(mean_t)
    q0 = state_start.reshape(FIELD)
    adjoint = adjoint_end.reshape(FIELD)
    narrow, wide = halved(LANES), halved(3 * LANES)
    both = [pltpu.VMEM((VARS * ROWS, 2 * LANES), BF16)]
    total = [pltpu.VMEM((VARS * ROWS, LANES), F32)]
    total3 = [pltpu.VMEM((VARS * ROWS, 3 * LANES), F32)]
    work = [pltpu.VMEM(FIELD, F32)]

    held = [q0, adjoint, reaction_rates, face_codes, limiter_flags, limiter_scales]
    held += [mean_t, forward]
    got = pl.pallas_call(
        functools.partial(start_kernel, len(held)),
        in_specs=[pl.BlockSpec(memory_space=pltpu.HBM)] * len(held),
        out_specs=[pl.BlockSpec(memory_space=pltpu.VMEM)] * (len(held) + 4),
        out_shape=[jax.ShapeDtypeStruct(v.shape, v.dtype) for v in held]
        + [jax.ShapeDtypeStruct(shape, F32) for shape in packs(1)],
        scratch_shapes=[pltpu.SemaphoreType.DMA((len(held),))],
        compiler_params=pltpu.CompilerParams(vmem_limit_bytes=8 << 20),
        name="start_kernel",
    )(*[pltpu.with_memory_space_constraint(v, pltpu.HBM) for v in held])
    q0, adjoint, rates, codes, flags, scales, mean_t, forward = got[: len(held)]
    got = exchange(got[len(held) :])
    size = functools.partial(setup_kernel, lax.axis_size("gx"), lax.axis_size("gy"))
    lam3, *along, walls, factors, coupling = call(
        size,
        [adjoint, rates, codes, flags, scales, mean_t],
        [FIELD] + packs(1) + [TABLE, TABLE, (SPECIES, SPECIES, LANES)],
        both,
    )

    def inner(mix, state):
        kernel = functools.partial(volume_kernel, mix)
        return call(kernel, [coupling, state, q0, walls, forward], [FIELD, FIELD], wide + total)

    def back_inner(state, lam, near):
        return call(
            back_volume_kernel, [coupling, state, lam, near, walls, backward], [FIELD], narrow + total3
        )[0]

    def outer(section, share, state, part, got, along=()):
        kernel = functools.partial(face_kernel, section, share, False)
        out, near_x, near_y, *sent = call(
            kernel, [state, part, walls, factors, mean, *got, *along],
            [FIELD] * 3 + packs(2 if along else 1),
            both,
        )
        return out, near_x, near_y, sent

    part, z0 = inner((0.0, 1.0), q0)
    q1, x0, y0, sent = outer(0, 1.0, q0, part, got)
    got = exchange(sent)
    part, z1 = inner((0.75, 0.25), q1)
    q2, x1, y1, sent = outer(1, 0.25, q1, part, got, along)
    got = exchange(sent)
    part, z2 = inner((1.0 / 3.0, 2.0 / 3.0), q2)
    back = back_inner(q2, lam3, z2)
    lam2, carry, x2, y2, *sent = call(
        turn_kernel,
        [q2, lam3, back, walls, factors, mean_t, *got],
        [FIELD] * 4 + packs(1),
        both + work,
    )
    got = exchange(sent)
    last = functools.partial(face_kernel, 2, 2.0 / 3.0, True)
    state_end = call(last, [q2, part, walls, factors, mean, x2, y2], [FIELD], both)[0]
    back = back_inner(q1, lam2, z1)
    lam1, *sent = call(
        middle_kernel,
        [q1, lam2, back, x1, y1, walls, factors, mean_t, *got],
        [FIELD] + packs(1),
        both + work,
    )
    got = exchange(sent)
    back = back_inner(q0, lam1, z0)
    adjoint_start = call(end_kernel, [q0, lam1, back, x0, y0, carry, walls, *got], [FIELD])[0]
    return state_end.reshape(state_start.shape), adjoint_start.reshape(state_start.shape)


def solution(mesh):
    field = P(None, "gx", "gy", None)
    return jax.shard_map(
        per_device,
        mesh=mesh,
        in_specs=(field, field, field, field, P("gx", "gy", None), P()),
        out_specs=(field, field),
        check_vma=False,
    )
```

```python
import functools

import jax
import jax.numpy as jnp
import numpy as np
from jax import lax
from jax.experimental import pallas as pl
from jax.experimental.pallas import tpu as pltpu
from jax.sharding import PartitionSpec as P

SPECIES = 21
VARS = 25
ENERGY = 24
GROUPS = 7
STEP = 0.008
F32 = jnp.float32
BF16 = jnp.bfloat16
ROWS = 16
LANES = 128


def node_tables():
    points = np.array([-1.0, -1.0 / np.sqrt(5.0), 1.0 / np.sqrt(5.0), 1.0])
    bary = np.array([1.0 / np.prod([points[a] - points[b] for b in range(4) if b != a]) for a in range(4)])
    deriv = np.zeros((4, 4))
    for a in range(4):
        for b in range(4):
            if a != b:
                deriv[a, b] = bary[b] / bary[a] / (points[a] - points[b])
        deriv[a, a] = -np.sum(deriv[a])
    eye = np.eye(4)
    pair = np.eye(2)
    ops = [
        np.kron(np.kron(deriv.T, eye), eye),
        np.kron(np.kron(eye, deriv.T), eye),
        np.kron(np.kron(eye, eye), deriv.T),
    ]
    grads = [np.kron(pair, op) for op in ops]
    whole = np.array([1.0, 5.0, 5.0, 1.0])
    cube = np.kron(np.kron(whole, whole), whole) / 2048.0
    mean = np.kron(pair, np.repeat(cube[:, None], 64, axis=1))
    forward = np.concatenate(grads, axis=0)
    backward = np.concatenate([g.T for g in grads], axis=1)
    return forward, backward, mean, mean.T


def stacked(table):
    return jnp.asarray(np.concatenate([table, table], axis=0).astype(jnp.bfloat16))


def halves(table):
    table = np.asarray(table, np.float32)
    high = table.astype(jnp.bfloat16)
    low = (table - high.astype(np.float32)).astype(jnp.bfloat16)
    return jnp.asarray(np.stack([high, low]))


def split(values):
    high = values.astype(BF16)
    return high, (values - high.astype(F32)).astype(BF16)


def product(high, low, table):
    dot = functools.partial(jnp.dot, preferred_element_type=F32)
    return dot(high, table[0]) + dot(high, table[1]) + dot(low, table[0])


def roll(values, shift, axis):
    shift = shift % values.shape[axis]
    return values if shift == 0 else pltpu.roll(values, shift, axis)


def lane_of(rows=ROWS):
    return lax.broadcasted_iota(jnp.int32, (rows, LANES), 1)


def node_index(direction, rows=ROWS):
    return (lane_of(rows) >> (4, 2, 0)[direction]) & 3


def block(var):
    return pl.ds(ROWS * var, ROWS)


class Face:
    def __init__(self, wall, direction):
        index = node_index(direction)
        inside = wall == 0.0
        self.low = jnp.logical_and(index == 0, inside)
        self.high = jnp.logical_and(index == 3, inside)
        self.sign = jnp.where(wall < 0.0, -1.0, 1.0)
        live = jnp.where(wall > 0.0, 0.0, 1.0)
        self.three = jnp.where(index == 0, 3.0, jnp.where(index == 3, -3.0, 0.0)) * live
        self.half = jnp.where(jnp.logical_or(index == 0, index == 3), 1.5, 0.0) * live
        self.momentum = SPECIES + direction

    def outside(self, var, own, low, high):
        edge = own * self.sign if var == self.momentum else own
        return jnp.where(self.low, low, jnp.where(self.high, high, edge))


def shift_z(values):
    first = lane_of() < 64
    low = roll(values, 61, 1)
    low = jnp.where(first, roll(low, 1, 0), low)
    high = roll(values, 67, 1)
    high = jnp.where(first, high, roll(high, ROWS - 1, 0))
    return low, high


def rows_of(ref, group, part):
    if group < GROUPS - 1:
        return pl.ds(ROWS * (part * (GROUPS - 1) + group), ROWS)
    parts = ref.shape[0] // 100
    return pl.ds(96 * parts + 4 * part, 4)


class Received:
    def __init__(self, refs, part=0):
        even_x = (jnp.zeros((8, LANES), jnp.int32) + lax.axis_index("gx") % 2) == 0
        even_y = (jnp.zeros((ROWS, LANES), jnp.int32) + lax.axis_index("gy") % 2) == 0
        yb, xb, ya, xa = refs
        self.packs = []
        for group in range(GROUPS):
            at = part * GROUPS + group
            a, b = xa[at], xb[at]
            c, d, even = *(ref[rows_of(ref, group, part), :] for ref in (ya, yb)), even_y
            if group == GROUPS - 1:
                even = even_y[:4]
            self.packs.append(
                (
                    jnp.where(even_x, b, a),
                    jnp.where(even_x, a, b),
                    jnp.where(even, d, c),
                    jnp.where(even, c, d),
                )
            )

    def along_x(self, var, own):
        group, slot = divmod(var, 4)
        low, high = self.packs[group][:2]
        first, second = own[:8], own[8:]
        return (
            jnp.concatenate([roll(low, -16 * slot, 1), roll(first, -48, 1)], axis=0),
            jnp.concatenate([roll(second, 48, 1), roll(high, 16 * (3 - slot), 1)], axis=0),
        )

    def along_y(self, var):
        group, slot = divmod(var, 4)
        low, high = self.packs[group][2:]
        if group == GROUPS - 1:
            return (
                jnp.concatenate([roll(low, -4 * k, 1) for k in range(4)], axis=0),
                jnp.concatenate([roll(high, 4 * (3 - k), 1) for k in range(4)], axis=0),
            )
        return roll(low, -4 * slot, 1), roll(high, 4 * (3 - slot), 1)


def pack(field, refs, part=0):
    even_x = (jnp.zeros((8, LANES), jnp.int32) + lax.axis_index("gx") % 2) == 0
    even_y = (jnp.zeros((ROWS, LANES), jnp.int32) + lax.axis_index("gy") % 2) == 0
    yb, xb, ya, xa = refs
    spot_x, spot_y = node_index(0, 8), node_index(1)

    def merged(spot, pieces):
        out = pieces[3]
        for slot in (2, 1, 0):
            out = jnp.where(spot == slot, pieces[slot], out)
        return out

    for group in range(GROUPS):
        at = part * GROUPS + group
        own = [field(min(4 * group + slot, ENERGY)) for slot in range(4)]
        if group == GROUPS - 1:
            x_low, x_high = own[0][:8], roll(own[0][8:], -48, 1)
            quarters = [own[0][4 * k : 4 * k + 4] for k in range(4)]
            y_low = merged(spot_y[:4], [roll(quarters[k], 4 * k, 1) for k in range(4)])
            y_high = merged(spot_y[:4], [roll(quarters[k], 4 * (k - 3), 1) for k in range(4)])
        else:
            x_low = merged(spot_x, [roll(own[s][:8], 16 * s, 1) for s in range(4)])
            x_high = merged(spot_x, [roll(own[s][8:], 16 * (s - 3), 1) for s in range(4)])
            y_low = merged(spot_y, [roll(own[s], 4 * s, 1) for s in range(4)])
            y_high = merged(spot_y, [roll(own[s], 4 * (s - 3), 1) for s in range(4)])
        xa[at] = jnp.where(even_x, x_high, x_low)
        xb[at] = jnp.where(even_x, x_low, x_high)
        even = even_y[:4] if group == GROUPS - 1 else even_y
        ya[rows_of(ya, group, part), :] = jnp.where(even, y_high, y_low)
        yb[rows_of(yb, group, part), :] = jnp.where(even, y_low, y_high)


class Gas:
    def __init__(self, field, directions):
        density = field(0)
        for var in range(1, SPECIES):
            density = density + field(var)
        self.inverse = 1.0 / density
        self.momenta = [field(SPECIES + e) for e in range(3)]
        m0, m1, m2 = self.momenta
        self.square = m0 * m0 + m1 * m1 + m2 * m2
        self.pressure = 0.4 * (field(ENERGY) - 0.5 * self.square * self.inverse)
        self.velocity = {d: self.momenta[d] * self.inverse for d in directions}
        sound = 1.4 * self.pressure * self.inverse
        self.speed = {d: jnp.sqrt(self.velocity[d] * self.velocity[d] + sound) for d in directions}


def face_gain(face, direction, own, other):
    weight = face.half * (own.speed[direction] + other.speed[direction])
    u_in, u_out = own.velocity[direction], other.velocity[direction]
    take, leave = face.three * u_out + weight, face.three * u_in + weight

    def gain(var, inside, outside):
        total = outside * take - inside * leave
        if var == face.momentum:
            total = total + face.three * (other.pressure - own.pressure)
        if var == ENERGY:
            total = total + face.three * (other.pressure * u_out - own.pressure * u_in)
        return total

    return gain


class Back:
    def __init__(self, gas):
        self.gas = gas
        zero = jnp.zeros((ROWS, LANES), F32)
        self.speed = {}
        self.velocity = {}
        self.pressure = zero

    def flux(self, var, direction, value, cotangent):
        gas = self.gas
        term = cotangent * value
        if var == ENERGY:
            term = term + cotangent * gas.pressure
            self.pressure = self.pressure + cotangent * gas.velocity[direction]
        if var == SPECIES + direction:
            self.pressure = self.pressure + cotangent
        held = self.velocity.get(direction)
        self.velocity[direction] = term if held is None else held + term
        return cotangent * gas.velocity[direction]

    def wave(self, direction, term):
        held = self.speed.get(direction)
        self.speed[direction] = term if held is None else held + term

    def close(self):
        gas = self.gas
        inverse, pressure = gas.inverse, self.pressure
        into = jnp.zeros((ROWS, LANES), F32)
        for direction, term in self.speed.items():
            scaled = term / gas.speed[direction]
            self.velocity[direction] = self.velocity[direction] + scaled * gas.velocity[direction]
            pressure = pressure + 0.7 * scaled * inverse
            into = into + 0.7 * scaled * gas.pressure
        for direction, term in self.velocity.items():
            into = into + term * gas.momenta[direction]
        into = into - 0.2 * pressure * gas.square
        self.species = -inverse * inverse * into
        self.momentum = []
        for e in range(3):
            term = -0.4 * pressure * gas.momenta[e]
            if e in self.velocity:
                term = term + self.velocity[e]
            self.momentum.append(term * inverse)
        self.energy = 0.4 * pressure

    def rest(self, var):
        if var < SPECIES:
            return self.species
        return self.energy if var == ENERGY else self.momentum[var - SPECIES]


def spread(lines):
    place = lax.broadcasted_iota(jnp.int32, (8, 16), 0)
    element = lax.broadcasted_iota(jnp.int32, (8, 16), 1)
    left = lane_of(8) < 64
    columns = []
    for column in range(2):
        line = jnp.broadcast_to(lines[column], (8, 16))
        picked = [
            jnp.sum(jnp.where(element == 2 * place + half, line, 0.0), axis=1, keepdims=True)
            for half in range(2)
        ]
        columns.append(jnp.where(left, picked[0], picked[1]))
    return jnp.concatenate(columns, axis=0)


def spread_rate(coupling, source, target):
    return jnp.broadcast_to(coupling[source, target : target + 1, :], (ROWS, LANES))


def damping(flags, scales, section):
    lines = []
    for column in range(2):
        at = (section, column)
        lines.append(jnp.where(flags[at] == 1, scales[at], 1.0))
    return spread(lines)


def limited(field, factor, both, table, transposed):
    for var in range(VARS):
        value = field(var)
        if transposed:
            value = (1.0 - factor) * value
        both[block(var), pl.ds(0, LANES)], both[block(var), pl.ds(LANES, LANES)] = split(value)
    means = jnp.dot(both[...], table[...], preferred_element_type=F32) * (2048.0 / 1728.0)

    def get(var):
        mean = means[ROWS * var : ROWS * (var + 1)]
        if transposed:
            return factor * field(var) + mean
        return mean + factor * (field(var) - mean)

    return get


def start_kernel(count, *refs):
    there, here, sent, arrived = refs[:count], refs[count : 2 * count], refs[2 * count : -1], refs[-1]
    copies = [pltpu.make_async_copy(there[k], here[k], arrived.at[k]) for k in range(count)]
    for copy in copies:
        copy.start()
    copies[0].wait()
    pack(lambda v: here[0][v], sent)
    for copy in copies[1:]:
        copy.wait()


def setup_kernel(columns, lines, adjoint, rates, codes, flags, scales, mean_t, lam, yb, xb, ya, xa, walls, factors, coupling, both):
    row = lax.broadcasted_iota(jnp.int32, (SPECIES, SPECIES), 0)
    same = row == lax.broadcasted_iota(jnp.int32, (SPECIES, SPECIES), 1)
    off_diag = jnp.where(same, 0.0, rates[...])
    leaving = jnp.sum(off_diag, axis=0, keepdims=True)
    full = jnp.where(same, -jnp.broadcast_to(leaving, (SPECIES, SPECIES)), off_diag)
    for source in range(SPECIES):
        coupling[source] = jnp.broadcast_to(full[:, source : source + 1], (SPECIES, LANES))
    for section in range(3):
        factors[section] = damping(flags, scales, section)
    get = limited(lambda v: adjoint[v], factors[2], both, mean_t, True)
    for var in range(VARS):
        lam[var] = (2.0 / 3.0) * get(var)
    pack(lambda v: lam[v], (yb, xb, ya, xa))
    code = spread([codes[column].astype(F32) for column in range(2)]).astype(jnp.int32)
    row = lax.broadcasted_iota(jnp.int32, (ROWS, LANES), 0)
    lane = lane_of()
    at_x = jnp.zeros((ROWS, LANES), jnp.int32) + lax.axis_index("gx")
    at_y = jnp.zeros((ROWS, LANES), jnp.int32) + lax.axis_index("gy")
    both = jnp.logical_and
    ends = (
        (both(at_x == 0, row < 8), both(at_x == columns - 1, row >= 8)),
        (at_y == 0, at_y == lines - 1),
        (both(row % 8 == 0, lane < 64), both(row % 8 == 7, lane >= 64)),
    )
    for d in range(3):
        index = node_index(d)
        low = (1 - 2 * ((code >> (2 * d)) & 1)).astype(F32)
        high = (1 - 2 * ((code >> (2 * d + 1)) & 1)).astype(F32)
        wall = jnp.where(both(ends[d][0], index == 0), low, 0.0)
        walls[d] = jnp.where(both(ends[d][1], index == 3), high, wall)


def volume_kernel(mix, coupling, state, start, walls, table, out, near, high, low, total):
    from_start, from_here = mix
    gas = Gas(lambda v: state[v], (0, 1, 2))
    for var in range(VARS):
        value = state[var]
        for d in range(3):
            flux = value * gas.velocity[d]
            if var == SPECIES + d:
                flux = flux + gas.pressure
            if var == ENERGY:
                flux = flux + gas.pressure * gas.velocity[d]
            at = pl.ds(LANES * d, LANES)
            high[block(var), at], low[block(var), at] = split(flux)
    total[...] = product(high[...], low[...], table)
    face = Face(walls[2], 2)
    for var in range(VARS):
        value = state[var]
        near[var] = face.outside(var, value, *shift_z(value))
    gain = face_gain(face, 2, gas, Gas(lambda v: near[v], (2,)))
    for var in range(VARS):
        value = state[var]
        change = gain(var, value, near[var]) - total[block(var), :]
        if var < SPECIES:
            for other in range(SPECIES):
                change = change + spread_rate(coupling, other, var) * state[other]
        here = from_here * value + (from_here * STEP) * change
        if from_start:
            here = here + from_start * start[var]
        out[var] = here


def fetch_near(state, walls, received, near_x, near_y):
    face_x, face_y = Face(walls[0], 0), Face(walls[1], 1)
    for var in range(VARS):
        value = state[var]
        near_x[var] = face_x.outside(var, value, *received.along_x(var, value))
        near_y[var] = face_y.outside(var, value, *received.along_y(var))


def face_kernel(section, share, last, state, inner, walls, factors, mean, *refs):
    along = ()
    if last:
        near_x, near_y, out, both = refs
    else:
        along = refs[4:-8]
        xa, xb, ya, yb = refs[:4]
        out, near_x, near_y, sa, sb, sc, sd, both = refs[-8:]
        fetch_near(state, walls, Received((xa, xb, ya, yb)), near_x, near_y)
    gas = Gas(lambda v: state[v], (0, 1))
    gain_x = face_gain(Face(walls[0], 0), 0, gas, Gas(lambda v: near_x[v], (0,)))
    gain_y = face_gain(Face(walls[1], 1), 1, gas, Gas(lambda v: near_y[v], (1,)))
    for var in range(VARS):
        value = state[var]
        change = gain_x(var, value, near_x[var]) + gain_y(var, value, near_y[var])
        out[var] = inner[var] + (share * STEP) * change
    get = limited(lambda v: out[v], factors[section], both, mean, False)
    for var in range(VARS):
        out[var] = get(var)
    if not last:
        pack(lambda v: out[v], (sa, sb, sc, sd))
        for held, sent in zip(along, (sa, sb, sc, sd)):
            if len(held.shape) == 3:
                sent[GROUPS:] = held[...]
            else:
                sent[96:192, :] = held[:96, :]
                sent[196:200, :] = held[96:100, :]


def back_volume_kernel(coupling, state, lam, near, walls, table, out, high, low, total):
    for var in range(VARS):
        high[block(var), :], low[block(var), :] = split(lam[var])
    total[...] = product(high[...], low[...], table)
    gas = Gas(lambda v: state[v], (0, 1, 2))
    other = Gas(lambda v: near[v], (2,))
    face = Face(walls[2], 2)
    speeds = gas.speed[2] + other.speed[2]
    back = Back(gas)
    for var in range(VARS):
        value, own = state[var], lam[var]
        outside = face.outside(var, own, *shift_z(own))
        part = back.flux(var, 0, value, -total[block(var), pl.ds(0, LANES)])
        part = part + back.flux(var, 1, value, -total[block(var), pl.ds(LANES, LANES)])
        part = part + back.flux(
            var, 2, value, -total[block(var), pl.ds(2 * LANES, LANES)] - face.three * (own + outside)
        )
        jump = face.half * (outside - own)
        back.wave(2, jump * (value - near[var]))
        out[var] = part + speeds * jump
    back.close()
    for var in range(VARS):
        change = out[var] + back.rest(var)
        if var < SPECIES:
            for other_var in range(SPECIES):
                change = change + spread_rate(coupling, var, other_var) * lam[other_var]
        out[var] = lam[var] + STEP * change


def back_faces(state, lam, near_x, near_y, walls, received, inner, out):
    gas = Gas(lambda v: state[v], (0, 1))
    faces = (Face(walls[0], 0), Face(walls[1], 1))
    nears = (near_x, near_y)
    speeds = [gas.speed[d] + Gas(lambda v, d=d: nears[d][v], (d,)).speed[d] for d in range(2)]
    back = Back(gas)
    for var in range(VARS):
        value, own = state[var], lam[var]
        part = inner[var]
        for d in range(2):
            sides = received.along_x(var, own) if d == 0 else received.along_y(var)
            outside = faces[d].outside(var, own, *sides)
            part = part + STEP * back.flux(var, d, value, -faces[d].three * (own + outside))
            jump = faces[d].half * (outside - own)
            back.wave(d, jump * (value - nears[d][var]))
            part = part + STEP * (speeds[d] * jump)
        out[var] = part
    back.close()
    for var in range(VARS):
        out[var] = out[var] + STEP * back.rest(var)


def turn_kernel(state, lam, inner, walls, factors, mean_t, *refs):
    got = refs[:4]
    below, carry, near_x, near_y, sa, sb, sc, sd, both, work = refs[4:]
    fetch_near(state, walls, Received(got), near_x, near_y)
    back_faces(state, lam, near_x, near_y, walls, Received(got, 1), inner, work)
    get = limited(lambda v: work[v], factors[1], both, mean_t, True)
    for var in range(VARS):
        reverse = get(var)
        carry[var] = 0.5 * lam[var] + 0.75 * reverse
        below[var] = 0.25 * reverse
    pack(lambda v: below[v], (sa, sb, sc, sd))


def middle_kernel(state, lam, inner, near_x, near_y, walls, factors, mean_t, *refs):
    la, lb, lc, ld, below, sa, sb, sc, sd, both, work = refs
    back_faces(state, lam, near_x, near_y, walls, Received((la, lb, lc, ld)), inner, work)
    get = limited(lambda v: work[v], factors[0], both, mean_t, True)
    for var in range(VARS):
        below[var] = get(var)
    pack(lambda v: below[v], (sa, sb, sc, sd))


def end_kernel(state, lam, inner, near_x, near_y, carry, walls, la, lb, lc, ld, out):
    back_faces(state, lam, near_x, near_y, walls, Received((la, lb, lc, ld)), inner, out)
    for var in range(VARS):
        out[var] = out[var] + carry[var]


FIELD = (VARS, ROWS, LANES)
TABLE = (3, ROWS, LANES)


def call(kernel, inputs, outputs, scratch=()):
    return pl.pallas_call(
        kernel,
        in_specs=[pl.BlockSpec(memory_space=pltpu.VMEM)] * len(inputs),
        out_specs=[pl.BlockSpec(memory_space=pltpu.VMEM)] * len(outputs),
        out_shape=[jax.ShapeDtypeStruct(shape, F32) for shape in outputs],
        scratch_shapes=list(scratch),
        compiler_params=pltpu.CompilerParams(vmem_limit_bytes=8 << 20),
        name=getattr(kernel, "func", kernel).__name__,
    )(*inputs)


def packs(parts):
    return [(parts * 100, LANES), (parts * GROUPS, 8, LANES), (parts * 100, LANES), (parts * GROUPS, 8, LANES)]


def halved(width):
    return [pltpu.VMEM((VARS * ROWS, width), BF16)] * 2


def exchange(sent):
    columns, lines = lax.axis_size("gx"), lax.axis_size("gy")

    def swap(values, along_x, first):
        moves = []
        for x in range(columns):
            for y in range(lines):
                at, count, other = (x, columns, y) if along_x else (y, lines, x)
                if at % 2 == first:
                    mate, across = at + 1, other
                else:
                    mate, across = at - 1, other
                if mate < 0 or mate >= count:
                    mate, across = at, other ^ 1
                to = (mate, across) if along_x else (across, mate)
                moves.append((x * lines + y, to[0] * lines + to[1]))
        return lax.ppermute(values, ("gx", "gy"), moves)

    yb, xb, ya, xa = sent
    yb = swap(yb, False, 1)
    xb = swap(xb, True, 1)
    ya = swap(ya, False, 0)
    xa = swap(xa, True, 0)
    return [yb, xb, ya, xa]


def per_device(state_start, adjoint_end, limiter_flags, limiter_scales, face_codes, reaction_rates):
    forward, backward, mean, mean_t = node_tables()
    forward, backward, mean, mean_t = halves(forward), halves(backward), stacked(mean), stacked(mean_t)
    q0 = state_start.reshape(FIELD)
    adjoint = adjoint_end.reshape(FIELD)
    narrow, wide = halved(LANES), halved(3 * LANES)
    both = [pltpu.VMEM((VARS * ROWS, 2 * LANES), BF16)]
    total = [pltpu.VMEM((VARS * ROWS, LANES), F32)]
    total3 = [pltpu.VMEM((VARS * ROWS, 3 * LANES), F32)]
    work = [pltpu.VMEM(FIELD, F32)]

    held = [q0, adjoint, reaction_rates, face_codes, limiter_flags, limiter_scales]
    held += [mean_t, forward]
    got = pl.pallas_call(
        functools.partial(start_kernel, len(held)),
        in_specs=[pl.BlockSpec(memory_space=pltpu.HBM)] * len(held),
        out_specs=[pl.BlockSpec(memory_space=pltpu.VMEM)] * (len(held) + 4),
        out_shape=[jax.ShapeDtypeStruct(v.shape, v.dtype) for v in held]
        + [jax.ShapeDtypeStruct(shape, F32) for shape in packs(1)],
        scratch_shapes=[pltpu.SemaphoreType.DMA((len(held),))],
        compiler_params=pltpu.CompilerParams(vmem_limit_bytes=8 << 20),
        name="start_kernel",
    )(*[pltpu.with_memory_space_constraint(v, pltpu.HBM) for v in held])
    q0, adjoint, rates, codes, flags, scales, mean_t, forward = got[: len(held)]
    got = exchange(got[len(held) :])
    size = functools.partial(setup_kernel, lax.axis_size("gx"), lax.axis_size("gy"))
    lam3, *along, walls, factors, coupling = call(
        size,
        [adjoint, rates, codes, flags, scales, mean_t],
        [FIELD] + packs(1) + [TABLE, TABLE, (SPECIES, SPECIES, LANES)],
        both,
    )

    def inner(mix, state):
        kernel = functools.partial(volume_kernel, mix)
        return call(kernel, [coupling, state, q0, walls, forward], [FIELD, FIELD], wide + total)

    def back_inner(state, lam, near):
        return call(
            back_volume_kernel, [coupling, state, lam, near, walls, backward], [FIELD], narrow + total3
        )[0]

    def outer(section, share, state, part, got, along=()):
        kernel = functools.partial(face_kernel, section, share, False)
        out, near_x, near_y, *sent = call(
            kernel, [state, part, walls, factors, mean, *got, *along],
            [FIELD] * 3 + packs(2 if along else 1),
            both,
        )
        return out, near_x, near_y, sent

    part, z0 = inner((0.0, 1.0), q0)
    q1, x0, y0, sent = outer(0, 1.0, q0, part, got)
    got = exchange(sent)
    part, z1 = inner((0.75, 0.25), q1)
    q2, x1, y1, sent = outer(1, 0.25, q1, part, got, along)
    got = exchange(sent)
    part, z2 = inner((1.0 / 3.0, 2.0 / 3.0), q2)
    back = back_inner(q2, lam3, z2)
    lam2, carry, x2, y2, *sent = call(
        turn_kernel,
        [q2, lam3, back, walls, factors, mean_t, *got],
        [FIELD] * 4 + packs(1),
        both + work,
    )
    got = exchange(sent)
    last = functools.partial(face_kernel, 2, 2.0 / 3.0, True)
    state_end = call(last, [q2, part, walls, factors, mean, x2, y2], [FIELD], both)[0]
    back = back_inner(q1, lam2, z1)
    lam1, *sent = call(
        middle_kernel,
        [q1, lam2, back, x1, y1, walls, factors, mean_t, *got],
        [FIELD] + packs(1),
        both + work,
    )
    got = exchange(sent)
    back = back_inner(q0, lam1, z0)
    adjoint_start = call(end_kernel, [q0, lam1, back, x0, y0, carry, walls, *got], [FIELD])[0]
    return state_end.reshape(state_start.shape), adjoint_start.reshape(state_start.shape)


def solution(mesh):
    field = P(None, "gx", "gy", None)
    return jax.shard_map(
        per_device,
        mesh=mesh,
        in_specs=(field, field, field, field, P("gx", "gy", None), P()),
        out_specs=(field, field),
        check_vma=False,
    )
```

```python
import functools

import jax
import jax.numpy as jnp
import numpy as np
from jax import lax
from jax.experimental import pallas as pl
from jax.experimental.pallas import tpu as pltpu
from jax.sharding import PartitionSpec as P

SPECIES = 21
VARS = 25
ENERGY = 24
GROUPS = 7
STEP = 0.008
F32 = jnp.float32
BF16 = jnp.bfloat16
ROWS = 16
LANES = 128


def node_tables():
    points = np.array([-1.0, -1.0 / np.sqrt(5.0), 1.0 / np.sqrt(5.0), 1.0])
    bary = np.array([1.0 / np.prod([points[a] - points[b] for b in range(4) if b != a]) for a in range(4)])
    deriv = np.zeros((4, 4))
    for a in range(4):
        for b in range(4):
            if a != b:
                deriv[a, b] = bary[b] / bary[a] / (points[a] - points[b])
        deriv[a, a] = -np.sum(deriv[a])
    eye = np.eye(4)
    pair = np.eye(2)
    ops = [
        np.kron(np.kron(deriv.T, eye), eye),
        np.kron(np.kron(eye, deriv.T), eye),
        np.kron(np.kron(eye, eye), deriv.T),
    ]
    grads = [np.kron(pair, op) for op in ops]
    whole = np.array([1.0, 5.0, 5.0, 1.0])
    cube = np.kron(np.kron(whole, whole), whole) / 2048.0
    mean = np.kron(pair, np.repeat(cube[:, None], 64, axis=1))
    forward = np.concatenate(grads, axis=0)
    backward = np.concatenate([g.T for g in grads], axis=1)
    return forward, backward, mean, mean.T


def stacked(table):
    return jnp.asarray(np.concatenate([table, table], axis=0).astype(jnp.bfloat16))


def halves(table):
    table = np.asarray(table, np.float32)
    high = table.astype(jnp.bfloat16)
    low = (table - high.astype(np.float32)).astype(jnp.bfloat16)
    return jnp.asarray(np.stack([high, low]))


def split(values):
    high = values.astype(BF16)
    return high, (values - high.astype(F32)).astype(BF16)


def product(high, low, table):
    dot = functools.partial(jnp.dot, preferred_element_type=F32)
    return dot(high, table[0]) + dot(high, table[1]) + dot(low, table[0])


def roll(values, shift, axis):
    shift = shift % values.shape[axis]
    return values if shift == 0 else pltpu.roll(values, shift, axis)


def lane_of(rows=ROWS):
    return lax.broadcasted_iota(jnp.int32, (rows, LANES), 1)


def node_index(direction, rows=ROWS):
    return (lane_of(rows) >> (4, 2, 0)[direction]) & 3


def block(var):
    return pl.ds(ROWS * var, ROWS)


class Face:
    def __init__(self, wall, direction):
        index = node_index(direction)
        inside = wall == 0.0
        self.low = jnp.logical_and(index == 0, inside)
        self.high = jnp.logical_and(index == 3, inside)
        self.sign = jnp.where(wall < 0.0, -1.0, 1.0)
        live = jnp.where(wall > 0.0, 0.0, 1.0)
        self.three = jnp.where(index == 0, 3.0, jnp.where(index == 3, -3.0, 0.0)) * live
        self.half = jnp.where(jnp.logical_or(index == 0, index == 3), 1.5, 0.0) * live
        self.momentum = SPECIES + direction

    def outside(self, var, own, low, high):
        edge = own * self.sign if var == self.momentum else own
        return jnp.where(self.low, low, jnp.where(self.high, high, edge))


def shift_z(values):
    first = lane_of() < 64
    low = roll(values, 61, 1)
    low = jnp.where(first, roll(low, 1, 0), low)
    high = roll(values, 67, 1)
    high = jnp.where(first, high, roll(high, ROWS - 1, 0))
    return low, high


def rows_of(ref, group, part):
    if group < GROUPS - 1:
        return pl.ds(ROWS * (part * (GROUPS - 1) + group), ROWS)
    parts = ref.shape[0] // 100
    return pl.ds(96 * parts + 4 * part, 4)


class Received:
    def __init__(self, refs, part=0):
        even_x = (jnp.zeros((8, LANES), jnp.int32) + lax.axis_index("gx") % 2) == 0
        even_y = (jnp.zeros((ROWS, LANES), jnp.int32) + lax.axis_index("gy") % 2) == 0
        yb, xb, ya, xa = refs
        self.packs = []
        for group in range(GROUPS):
            at = part * GROUPS + group
            a, b = xa[at], xb[at]
            c, d, even = *(ref[rows_of(ref, group, part), :] for ref in (ya, yb)), even_y
            if group == GROUPS - 1:
                even = even_y[:4]
            self.packs.append(
                (
                    jnp.where(even_x, b, a),
                    jnp.where(even_x, a, b),
                    jnp.where(even, d, c),
                    jnp.where(even, c, d),
                )
            )

    def along_x(self, var, own):
        group, slot = divmod(var, 4)
        low, high = self.packs[group][:2]
        first, second = own[:8], own[8:]
        return (
            jnp.concatenate([roll(low, -16 * slot, 1), roll(first, -48, 1)], axis=0),
            jnp.concatenate([roll(second, 48, 1), roll(high, 16 * (3 - slot), 1)], axis=0),
        )

    def along_y(self, var):
        group, slot = divmod(var, 4)
        low, high = self.packs[group][2:]
        if group == GROUPS - 1:
            return (
                jnp.concatenate([roll(low, -4 * k, 1) for k in range(4)], axis=0),
                jnp.concatenate([roll(high, 4 * (3 - k), 1) for k in range(4)], axis=0),
            )
        return roll(low, -4 * slot, 1), roll(high, 4 * (3 - slot), 1)


def pack(field, refs, part=0):
    even_x = (jnp.zeros((8, LANES), jnp.int32) + lax.axis_index("gx") % 2) == 0
    even_y = (jnp.zeros((ROWS, LANES), jnp.int32) + lax.axis_index("gy") % 2) == 0
    yb, xb, ya, xa = refs
    spot_x, spot_y = node_index(0, 8), node_index(1)

    def merged(spot, pieces):
        out = pieces[3]
        for slot in (2, 1, 0):
            out = jnp.where(spot == slot, pieces[slot], out)
        return out

    for group in range(GROUPS):
        at = part * GROUPS + group
        own = [field(min(4 * group + slot, ENERGY)) for slot in range(4)]
        if group == GROUPS - 1:
            x_low, x_high = own[0][:8], roll(own[0][8:], -48, 1)
            quarters = [own[0][4 * k : 4 * k + 4] for k in range(4)]
            y_low = merged(spot_y[:4], [roll(quarters[k], 4 * k, 1) for k in range(4)])
            y_high = merged(spot_y[:4], [roll(quarters[k], 4 * (k - 3), 1) for k in range(4)])
        else:
            x_low = merged(spot_x, [roll(own[s][:8], 16 * s, 1) for s in range(4)])
            x_high = merged(spot_x, [roll(own[s][8:], 16 * (s - 3), 1) for s in range(4)])
            y_low = merged(spot_y, [roll(own[s], 4 * s, 1) for s in range(4)])
            y_high = merged(spot_y, [roll(own[s], 4 * (s - 3), 1) for s in range(4)])
        xa[at] = jnp.where(even_x, x_high, x_low)
        xb[at] = jnp.where(even_x, x_low, x_high)
        even = even_y[:4] if group == GROUPS - 1 else even_y
        ya[rows_of(ya, group, part), :] = jnp.where(even, y_high, y_low)
        yb[rows_of(yb, group, part), :] = jnp.where(even, y_low, y_high)


class Gas:
    def __init__(self, field, directions):
        density = field(0)
        for var in range(1, SPECIES):
            density = density + field(var)
        self.inverse = 1.0 / density
        self.momenta = [field(SPECIES + e) for e in range(3)]
        m0, m1, m2 = self.momenta
        self.square = m0 * m0 + m1 * m1 + m2 * m2
        self.pressure = 0.4 * (field(ENERGY) - 0.5 * self.square * self.inverse)
        self.velocity = {d: self.momenta[d] * self.inverse for d in directions}
        sound = 1.4 * self.pressure * self.inverse
        self.speed = {d: jnp.sqrt(self.velocity[d] * self.velocity[d] + sound) for d in directions}


def face_gain(face, direction, own, other):
    weight = face.half * (own.speed[direction] + other.speed[direction])
    u_in, u_out = own.velocity[direction], other.velocity[direction]
    take, leave = face.three * u_out + weight, face.three * u_in + weight

    def gain(var, inside, outside):
        total = outside * take - inside * leave
        if var == face.momentum:
            total = total + face.three * (other.pressure - own.pressure)
        if var == ENERGY:
            total = total + face.three * (other.pressure * u_out - own.pressure * u_in)
        return total

    return gain


class Back:
    def __init__(self, gas):
        self.gas = gas
        zero = jnp.zeros((ROWS, LANES), F32)
        self.speed = {}
        self.velocity = {}
        self.pressure = zero

    def flux(self, var, direction, value, cotangent):
        gas = self.gas
        term = cotangent * value
        if var == ENERGY:
            term = term + cotangent * gas.pressure
            self.pressure = self.pressure + cotangent * gas.velocity[direction]
        if var == SPECIES + direction:
            self.pressure = self.pressure + cotangent
        held = self.velocity.get(direction)
        self.velocity[direction] = term if held is None else held + term
        return cotangent * gas.velocity[direction]

    def wave(self, direction, term):
        held = self.speed.get(direction)
        self.speed[direction] = term if held is None else held + term

    def close(self):
        gas = self.gas
        inverse, pressure = gas.inverse, self.pressure
        into = jnp.zeros((ROWS, LANES), F32)
        for direction, term in self.speed.items():
            scaled = term / gas.speed[direction]
            self.velocity[direction] = self.velocity[direction] + scaled * gas.velocity[direction]
            pressure = pressure + 0.7 * scaled * inverse
            into = into + 0.7 * scaled * gas.pressure
        for direction, term in self.velocity.items():
            into = into + term * gas.momenta[direction]
        into = into - 0.2 * pressure * gas.square
        self.species = -inverse * inverse * into
        self.momentum = []
        for e in range(3):
            term = -0.4 * pressure * gas.momenta[e]
            if e in self.velocity:
                term = term + self.velocity[e]
            self.momentum.append(term * inverse)
        self.energy = 0.4 * pressure

    def rest(self, var):
        if var < SPECIES:
            return self.species
        return self.energy if var == ENERGY else self.momentum[var - SPECIES]


def spread(lines):
    place = lax.broadcasted_iota(jnp.int32, (8, 16), 0)
    element = lax.broadcasted_iota(jnp.int32, (8, 16), 1)
    left = lane_of(8) < 64
    columns = []
    for column in range(2):
        line = jnp.broadcast_to(lines[column], (8, 16))
        picked = [
            jnp.sum(jnp.where(element == 2 * place + half, line, 0.0), axis=1, keepdims=True)
            for half in range(2)
        ]
        columns.append(jnp.where(left, picked[0], picked[1]))
    return jnp.concatenate(columns, axis=0)


def spread_rate(coupling, source, target):
    return jnp.broadcast_to(coupling[source, target : target + 1, :], (ROWS, LANES))


def damping(flags, scales, section):
    lines = []
    for column in range(2):
        at = (section, column)
        lines.append(jnp.where(flags[at] == 1, scales[at], 1.0))
    return spread(lines)


def limited(field, factor, both, table, transposed):
    for var in range(VARS):
        value = field(var)
        if transposed:
            value = (1.0 - factor) * value
        both[block(var), pl.ds(0, LANES)], both[block(var), pl.ds(LANES, LANES)] = split(value)
    means = jnp.dot(both[...], table[...], preferred_element_type=F32) * (2048.0 / 1728.0)

    def get(var):
        mean = means[ROWS * var : ROWS * (var + 1)]
        if transposed:
            return factor * field(var) + mean
        return mean + factor * (field(var) - mean)

    return get


def start_kernel(count, *refs):
    there, here, sent, arrived = refs[:count], refs[count : 2 * count], refs[2 * count : -1], refs[-1]
    copies = [pltpu.make_async_copy(there[k], here[k], arrived.at[k]) for k in range(count)]
    for copy in copies:
        copy.start()
    copies[0].wait()
    pack(lambda v: here[0][v], sent)
    for copy in copies[1:]:
        copy.wait()


def setup_kernel(columns, lines, adjoint, rates, codes, flags, scales, mean_t, lam, yb, xb, ya, xa, walls, factors, coupling, both):
    row = lax.broadcasted_iota(jnp.int32, (SPECIES, SPECIES), 0)
    same = row == lax.broadcasted_iota(jnp.int32, (SPECIES, SPECIES), 1)
    off_diag = jnp.where(same, 0.0, rates[...])
    leaving = jnp.sum(off_diag, axis=0, keepdims=True)
    full = jnp.where(same, -jnp.broadcast_to(leaving, (SPECIES, SPECIES)), off_diag)
    for source in range(SPECIES):
        coupling[source] = jnp.broadcast_to(full[:, source : source + 1], (SPECIES, LANES))
    for section in range(3):
        factors[section] = damping(flags, scales, section)
    get = limited(lambda v: adjoint[v], factors[2], both, mean_t, True)
    for var in range(VARS):
        lam[var] = (2.0 / 3.0) * get(var)
    pack(lambda v: lam[v], (yb, xb, ya, xa))
    code = spread([codes[column].astype(F32) for column in range(2)]).astype(jnp.int32)
    row = lax.broadcasted_iota(jnp.int32, (ROWS, LANES), 0)
    lane = lane_of()
    at_x = jnp.zeros((ROWS, LANES), jnp.int32) + lax.axis_index("gx")
    at_y = jnp.zeros((ROWS, LANES), jnp.int32) + lax.axis_index("gy")
    both = jnp.logical_and
    ends = (
        (both(at_x == 0, row < 8), both(at_x == columns - 1, row >= 8)),
        (at_y == 0, at_y == lines - 1),
        (both(row % 8 == 0, lane < 64), both(row % 8 == 7, lane >= 64)),
    )
    for d in range(3):
        index = node_index(d)
        low = (1 - 2 * ((code >> (2 * d)) & 1)).astype(F32)
        high = (1 - 2 * ((code >> (2 * d + 1)) & 1)).astype(F32)
        wall = jnp.where(both(ends[d][0], index == 0), low, 0.0)
        walls[d] = jnp.where(both(ends[d][1], index == 3), high, wall)


def volume_kernel(mix, coupling, state, start, walls, table, out, near, high, low, total):
    from_start, from_here = mix
    gas = Gas(lambda v: state[v], (0, 1, 2))
    for var in range(VARS):
        value = state[var]
        for d in range(3):
            flux = value * gas.velocity[d]
            if var == SPECIES + d:
                flux = flux + gas.pressure
            if var == ENERGY:
                flux = flux + gas.pressure * gas.velocity[d]
            at = pl.ds(LANES * d, LANES)
            high[block(var), at], low[block(var), at] = split(flux)
    total[...] = product(high[...], low[...], table)
    face = Face(walls[2], 2)
    for var in range(VARS):
        value = state[var]
        near[var] = face.outside(var, value, *shift_z(value))
    gain = face_gain(face, 2, gas, Gas(lambda v: near[v], (2,)))
    for var in range(VARS):
        value = state[var]
        change = gain(var, value, near[var]) - total[block(var), :]
        if var < SPECIES:
            for other in range(SPECIES):
                change = change + spread_rate(coupling, other, var) * state[other]
        here = from_here * value + (from_here * STEP) * change
        if from_start:
            here = here + from_start * start[var]
        out[var] = here


def fetch_near(state, walls, received, near_x, near_y):
    face_x, face_y = Face(walls[0], 0), Face(walls[1], 1)
    for var in range(VARS):
        value = state[var]
        near_x[var] = face_x.outside(var, value, *received.along_x(var, value))
        near_y[var] = face_y.outside(var, value, *received.along_y(var))


def face_kernel(section, share, last, state, inner, walls, factors, mean, *refs):
    along = ()
    if last:
        near_x, near_y, out, both = refs
    else:
        along = refs[4:-8]
        xa, xb, ya, yb = refs[:4]
        out, near_x, near_y, sa, sb, sc, sd, both = refs[-8:]
        fetch_near(state, walls, Received((xa, xb, ya, yb)), near_x, near_y)
    gas = Gas(lambda v: state[v], (0, 1))
    gain_x = face_gain(Face(walls[0], 0), 0, gas, Gas(lambda v: near_x[v], (0,)))
    gain_y = face_gain(Face(walls[1], 1), 1, gas, Gas(lambda v: near_y[v], (1,)))
    for var in range(VARS):
        value = state[var]
        change = gain_x(var, value, near_x[var]) + gain_y(var, value, near_y[var])
        out[var] = inner[var] + (share * STEP) * change
    get = limited(lambda v: out[v], factors[section], both, mean, False)
    for var in range(VARS):
        out[var] = get(var)
    if not last:
        pack(lambda v: out[v], (sa, sb, sc, sd))
        for held, sent in zip(along, (sa, sb, sc, sd)):
            if len(held.shape) == 3:
                sent[GROUPS:] = held[...]
            else:
                sent[96:192, :] = held[:96, :]
                sent[196:200, :] = held[96:100, :]


def back_volume_kernel(coupling, state, lam, near, walls, table, out, high, low, total):
    for var in range(VARS):
        high[block(var), :], low[block(var), :] = split(lam[var])
    total[...] = product(high[...], low[...], table)
    gas = Gas(lambda v: state[v], (0, 1, 2))
    other = Gas(lambda v: near[v], (2,))
    face = Face(walls[2], 2)
    speeds = gas.speed[2] + other.speed[2]
    back = Back(gas)
    for var in range(VARS):
        value, own = state[var], lam[var]
        outside = face.outside(var, own, *shift_z(own))
        part = back.flux(var, 0, value, -total[block(var), pl.ds(0, LANES)])
        part = part + back.flux(var, 1, value, -total[block(var), pl.ds(LANES, LANES)])
        part = part + back.flux(
            var, 2, value, -total[block(var), pl.ds(2 * LANES, LANES)] - face.three * (own + outside)
        )
        jump = face.half * (outside - own)
        back.wave(2, jump * (value - near[var]))
        out[var] = part + speeds * jump
    back.close()
    for var in range(VARS):
        change = out[var] + back.rest(var)
        if var < SPECIES:
            for other_var in range(SPECIES):
                change = change + spread_rate(coupling, var, other_var) * lam[other_var]
        out[var] = lam[var] + STEP * change


def back_faces(state, lam, near_x, near_y, walls, received, inner, out, carry=None):
    gas = Gas(lambda v: state[v], (0, 1))
    faces = (Face(walls[0], 0), Face(walls[1], 1))
    nears = (near_x, near_y)
    speeds = [gas.speed[d] + Gas(lambda v, d=d: nears[d][v], (d,)).speed[d] for d in range(2)]
    back = Back(gas)
    for var in range(VARS):
        value, own = state[var], lam[var]
        part = inner[var]
        for d in range(2):
            sides = received.along_x(var, own) if d == 0 else received.along_y(var)
            outside = faces[d].outside(var, own, *sides)
            part = part + STEP * back.flux(var, d, value, -faces[d].three * (own + outside))
            jump = faces[d].half * (outside - own)
            back.wave(d, jump * (value - nears[d][var]))
            part = part + STEP * (speeds[d] * jump)
        out[var] = part
    back.close()
    for var in range(VARS):
        total = out[var] + STEP * back.rest(var)
        out[var] = total if carry is None else total + carry[var]


def turn_kernel(state, lam, inner, walls, factors, mean_t, *refs):
    got = refs[:4]
    below, carry, near_x, near_y, sa, sb, sc, sd, both, work = refs[4:]
    fetch_near(state, walls, Received(got), near_x, near_y)
    back_faces(state, lam, near_x, near_y, walls, Received(got, 1), inner, work)
    get = limited(lambda v: work[v], factors[1], both, mean_t, True)
    for var in range(VARS):
        reverse = get(var)
        carry[var] = 0.5 * lam[var] + 0.75 * reverse
        below[var] = 0.25 * reverse
    pack(lambda v: below[v], (sa, sb, sc, sd))


def middle_kernel(state, lam, inner, near_x, near_y, walls, factors, mean_t, *refs):
    la, lb, lc, ld, below, sa, sb, sc, sd, both, work = refs
    back_faces(state, lam, near_x, near_y, walls, Received((la, lb, lc, ld)), inner, work)
    get = limited(lambda v: work[v], factors[0], both, mean_t, True)
    for var in range(VARS):
        below[var] = get(var)
    pack(lambda v: below[v], (sa, sb, sc, sd))


def end_kernel(state, lam, inner, near_x, near_y, carry, walls, la, lb, lc, ld, out):
    back_faces(state, lam, near_x, near_y, walls, Received((la, lb, lc, ld)), inner, out, carry)


FIELD = (VARS, ROWS, LANES)
TABLE = (3, ROWS, LANES)


def call(kernel, inputs, outputs, scratch=()):
    return pl.pallas_call(
        kernel,
        in_specs=[pl.BlockSpec(memory_space=pltpu.VMEM)] * len(inputs),
        out_specs=[pl.BlockSpec(memory_space=pltpu.VMEM)] * len(outputs),
        out_shape=[jax.ShapeDtypeStruct(shape, F32) for shape in outputs],
        scratch_shapes=list(scratch),
        compiler_params=pltpu.CompilerParams(vmem_limit_bytes=8 << 20),
        name=getattr(kernel, "func", kernel).__name__,
    )(*inputs)


def packs(parts):
    return [(parts * 100, LANES), (parts * GROUPS, 8, LANES), (parts * 100, LANES), (parts * GROUPS, 8, LANES)]


def halved(width):
    return [pltpu.VMEM((VARS * ROWS, width), BF16)] * 2


def exchange(sent):
    columns, lines = lax.axis_size("gx"), lax.axis_size("gy")

    def swap(values, along_x, first):
        moves = []
        for x in range(columns):
            for y in range(lines):
                at, count, other = (x, columns, y) if along_x else (y, lines, x)
                if at % 2 == first:
                    mate, across = at + 1, other
                else:
                    mate, across = at - 1, other
                if mate < 0 or mate >= count:
                    mate, across = at, other ^ 1
                to = (mate, across) if along_x else (across, mate)
                moves.append((x * lines + y, to[0] * lines + to[1]))
        return lax.ppermute(values, ("gx", "gy"), moves)

    yb, xb, ya, xa = sent
    yb = swap(yb, False, 1)
    xb = swap(xb, True, 1)
    ya = swap(ya, False, 0)
    xa = swap(xa, True, 0)
    return [yb, xb, ya, xa]


def per_device(state_start, adjoint_end, limiter_flags, limiter_scales, face_codes, reaction_rates):
    forward, backward, mean, mean_t = node_tables()
    forward, backward, mean, mean_t = halves(forward), halves(backward), stacked(mean), stacked(mean_t)
    q0 = state_start.reshape(FIELD)
    adjoint = adjoint_end.reshape(FIELD)
    narrow, wide = halved(LANES), halved(3 * LANES)
    both = [pltpu.VMEM((VARS * ROWS, 2 * LANES), BF16)]
    total = [pltpu.VMEM((VARS * ROWS, LANES), F32)]
    total3 = [pltpu.VMEM((VARS * ROWS, 3 * LANES), F32)]
    work = [pltpu.VMEM(FIELD, F32)]

    held = [q0, adjoint, reaction_rates, face_codes, limiter_flags, limiter_scales]
    held += [mean_t]
    got = pl.pallas_call(
        functools.partial(start_kernel, len(held)),
        in_specs=[pl.BlockSpec(memory_space=pltpu.HBM)] * len(held),
        out_specs=[pl.BlockSpec(memory_space=pltpu.VMEM)] * (len(held) + 4),
        out_shape=[jax.ShapeDtypeStruct(v.shape, v.dtype) for v in held]
        + [jax.ShapeDtypeStruct(shape, F32) for shape in packs(1)],
        scratch_shapes=[pltpu.SemaphoreType.DMA((len(held),))],
        compiler_params=pltpu.CompilerParams(vmem_limit_bytes=8 << 20),
        name="start_kernel",
    )(*[pltpu.with_memory_space_constraint(v, pltpu.HBM) for v in held])
    q0, adjoint, rates, codes, flags, scales, mean_t = got[: len(held)]
    got = exchange(got[len(held) :])
    size = functools.partial(setup_kernel, lax.axis_size("gx"), lax.axis_size("gy"))
    lam3, *along, walls, factors, coupling = call(
        size,
        [adjoint, rates, codes, flags, scales, mean_t],
        [FIELD] + packs(1) + [TABLE, TABLE, (SPECIES, SPECIES, LANES)],
        both,
    )

    def inner(mix, state):
        kernel = functools.partial(volume_kernel, mix)
        return call(kernel, [coupling, state, q0, walls, forward], [FIELD, FIELD], wide + total)

    def back_inner(state, lam, near):
        return call(
            back_volume_kernel, [coupling, state, lam, near, walls, backward], [FIELD], narrow + total3
        )[0]

    def outer(section, share, state, part, got, along=()):
        kernel = functools.partial(face_kernel, section, share, False)
        out, near_x, near_y, *sent = call(
            kernel, [state, part, walls, factors, mean, *got, *along],
            [FIELD] * 3 + packs(2 if along else 1),
            both,
        )
        return out, near_x, near_y, sent

    part, z0 = inner((0.0, 1.0), q0)
    q1, x0, y0, sent = outer(0, 1.0, q0, part, got)
    got = exchange(sent)
    part, z1 = inner((0.75, 0.25), q1)
    q2, x1, y1, sent = outer(1, 0.25, q1, part, got, along)
    got = exchange(sent)
    part, z2 = inner((1.0 / 3.0, 2.0 / 3.0), q2)
    back = back_inner(q2, lam3, z2)
    lam2, carry, x2, y2, *sent = call(
        turn_kernel,
        [q2, lam3, back, walls, factors, mean_t, *got],
        [FIELD] * 4 + packs(1),
        both + work,
    )
    got = exchange(sent)
    last = functools.partial(face_kernel, 2, 2.0 / 3.0, True)
    state_end = call(last, [q2, part, walls, factors, mean, x2, y2], [FIELD], both)[0]
    back = back_inner(q1, lam2, z1)
    lam1, *sent = call(
        middle_kernel,
        [q1, lam2, back, x1, y1, walls, factors, mean_t, *got],
        [FIELD] + packs(1),
        both + work,
    )
    got = exchange(sent)
    back = back_inner(q0, lam1, z0)
    adjoint_start = call(end_kernel, [q0, lam1, back, x0, y0, carry, walls, *got], [FIELD])[0]
    return state_end.reshape(state_start.shape), adjoint_start.reshape(state_start.shape)


def solution(mesh):
    field = P(None, "gx", "gy", None)
    return jax.shard_map(
        per_device,
        mesh=mesh,
        in_specs=(field, field, field, field, P("gx", "gy", None), P()),
        out_specs=(field, field),
        check_vma=False,
    )
```
